256 devices in a mesh: dp: 32 (over x, z_hi, core), tensor: 8 (over y, z_lo).
Axes of the slice: x: 4, y: 4, z: 8 (z_hi: 4, z_lo: 2; z = z_hi * 2 + z_lo), core: 2. Of those that a mesh axis runs over, the one named last changes fastest.
Arguments:
- activations: bfloat16 [32768, 2880], P(('dp', 'tensor')), parts along dimension 0, may hold values from -6 to 6
- segment_ids: int32 [32768], P('dp'), parts along dimension 0, may hold values from 0 to 3, as said below
- attn_gain: float32 [2880], replicated, may hold values from 0.1 to 1.9
- qkv_weight: bfloat16 [2880, 5120], P(None, 'tensor'), may hold values from -2 to 2
- out_weight: bfloat16 [4096, 2880], P('tensor'), may hold values from -0.09375 to 0.09375
- ffn_gain: float32 [2880], replicated, may hold values from 0.1 to 1.9
- gate_weight: bfloat16 [2880, 2048], P(None, 'tensor'), may hold values from -0.109375 to 0.109375
- up_weight: bfloat16 [2880, 2048], P(None, 'tensor'), may hold values from -0.109375 to 0.109375
- down_weight: bfloat16 [2048, 2880], P('tensor'), may hold values from -0.125 to 0.125
Outputs:
- layer_out: bfloat16 [32768, 2880], P(('dp', 'tensor')), parts along dimension 0
The draws below stay inside these ranges and needn't reach their ends.
There are 32 independent parts, one for each index of `dp`. The reference program is written for one: setup_inputs(seed, part) draws one part's arguments, and reference() takes and returns one part's arrays. A program takes and returns all parts, laid end to end along the dimension named above; an argument that names none is the same for every part. Nothing has to cross between parts.
Inputs may be any that keep to these rules, and one draw needn't show every extreme that they name: `segment_ids`: segment numbers never fall along the tokens, and each of the four segments holds at least one token.
All inputs are finite; a program needn't handle non-finite values.
Results may differ from the reference program's by a relative error of at most 0.035.
Values may be sent and summed in bfloat16 or wider, within the bound.
A program may use at most 128 MiB of HBM per device.

```python
import jax
import jax.numpy as jnp
from jax import lax

D = 2880
HEADS = 64
KV_HEADS = 8
HEAD_DIM = 64
FF = 2048
TOKENS = 1024
N_TENSOR = 8


def draw_segment_ids(key, part):
    cut_key = jax.random.fold_in(key, 7103)
    cuts = jax.random.permutation(cut_key, TOKENS - 1)[:3].astype(jnp.int32) + 1
    positions = jnp.arange(TOKENS, dtype=jnp.int32)
    above = (positions[:, None] >= cuts[None, :]).astype(jnp.int32)
    return jnp.sum(above, axis=1).astype(jnp.int32)


def draw_qkv_weight(key, part):
    width = (HEADS // KV_HEADS + 2) * HEAD_DIM
    first_key = jax.random.fold_in(key, 0)
    base = jnp.clip(jax.random.normal(first_key, (D, KV_HEADS, width), jnp.float32), -6.0, 6.0) * D ** (-0.5)
    return base.reshape(D, KV_HEADS * width).astype(jnp.bfloat16)


def block_levels(rng, shape, shards, smallest, top_value):
    def one(axis_at, blocks):
        heights = jax.random.uniform(jax.random.fold_in(jax.random.fold_in(rng, 6), axis_at), (blocks,), jnp.float32, smallest / len(shards), top_value / len(shards))
        return jnp.repeat(jnp.exp(heights), shape[axis_at] // blocks).reshape((-1,) + (1,) * (len(shape) - axis_at - 1))

    factor_of = one(*shards[0])
    for cut in shards[1:]:
        factor_of = factor_of * one(*cut)
    return factor_of


def normal_values(rng, dims, spread, bound, cuts=(), kind=jnp.bfloat16):
    values = jax.random.normal(rng, dims, jnp.float32) * spread
    if len(cuts) > 0:
        values = block_levels(rng, dims, cuts, -0.22, 0.18) * values
    return jnp.clip(values, min=-bound, max=bound).astype(kind)


def setup_inputs(seed: int = 0, part: int = 0) -> dict:
    streams_of = jax.random.split(jax.random.key(seed), 10)
    part_splits = jax.random.split(jax.random.fold_in(streams_of[9], part), 10)
    return {
        "activations": normal_values(part_splits[0], (TOKENS, D), 1.0, 6.0, ((0, 8),)),
        "segment_ids": draw_segment_ids(jax.random.fold_in(jax.random.fold_in(streams_of[9], part), 71), part),
        "attn_gain": jnp.clip(1.0 + 0.18 * jax.random.normal(streams_of[2], (D,), jnp.float32), 0.1, 1.9),
        "qkv_weight": draw_qkv_weight(jax.random.fold_in(streams_of[9], 71), part),
        "out_weight": normal_values(streams_of[4], (HEADS * HEAD_DIM, D), (HEADS * HEAD_DIM) ** -0.5, 0.09375, ((0, 8),)),
        "ffn_gain": jnp.clip(1.0 + 0.18 * jax.random.normal(streams_of[5], (D,), jnp.float32), 0.1, 1.9),
        "gate_weight": normal_values(streams_of[6], (D, FF), D ** -0.5, 0.109375, ((1, 8),)),
        "up_weight": normal_values(streams_of[7], (D, FF), D ** -0.5, 0.109375, ((1, 8),)),
        "down_weight": normal_values(streams_of[8], (FF, D), FF ** -0.5, 0.125, ((0, 8),)),
    }


def normalize(rows_in, gain):
    floats = rows_in.astype(jnp.float32)
    mean_square = lax.optimization_barrier(jnp.mean(floats * floats, axis=-1, keepdims=True))
    return (floats * lax.rsqrt(mean_square + 1e-05) * gain).astype(jnp.bfloat16)

def grouped_sum(left, right):
    group_rows = right.shape[0] // N_TENSOR
    total = jnp.zeros((left.shape[0], right.shape[1]), jnp.float32)
    for group in range(N_TENSOR):
        part_left = left[:, group * group_rows:(group + 1) * group_rows]
        part_right = right[group * group_rows:(group + 1) * group_rows]
        partial_out = jnp.dot(part_left, part_right, preferred_element_type=jnp.float32).astype(jnp.bfloat16)
        total = total + partial_out.astype(jnp.float32)
    return total

def reference(activations, segment_ids, attn_gain, qkv_weight, out_weight, ffn_gain, gate_weight, up_weight, down_weight):
    group_size = HEADS // KV_HEADS
    normed = normalize(activations, attn_gain)
    projected = jnp.dot(normed, qkv_weight, preferred_element_type=jnp.float32).astype(jnp.bfloat16)
    projected = projected.reshape(TOKENS, KV_HEADS, group_size + 2, HEAD_DIM)
    queries = projected[:, :, :group_size].astype(jnp.float32)
    key_rows = projected[:, :, group_size].astype(jnp.float32)
    value_rows = projected[:, :, group_size + 1].astype(jnp.float32)
    scores = jnp.einsum('sngd,tnd->ngst', queries, key_rows) * HEAD_DIM ** (-0.5)
    positions = jnp.arange(TOKENS, dtype=jnp.int32)
    allowed = (positions[None, :] <= positions[:, None]) & (segment_ids[None, :] == segment_ids[:, None])
    scores = jnp.where(allowed, scores, -1e+30)
    row_max = lax.optimization_barrier(jnp.max(scores, axis=-1, keepdims=True))
    weights = jnp.exp(scores - row_max)
    row_total = lax.optimization_barrier(jnp.sum(weights, axis=-1, keepdims=True))
    softmax_out = lax.optimization_barrier((weights / row_total).astype(jnp.bfloat16))
    mixed = jnp.einsum('ngst,tnd->sngd', softmax_out.astype(jnp.float32), value_rows)
    mixed_heads = mixed.astype(jnp.bfloat16).reshape(TOKENS, HEADS * HEAD_DIM)
    attn_proj = grouped_sum(mixed_heads, out_weight)
    resid_sum = (activations.astype(jnp.float32) + attn_proj).astype(jnp.bfloat16)
    ffn_input = normalize(resid_sum, ffn_gain)
    gate_act = jnp.dot(ffn_input, gate_weight, preferred_element_type=jnp.float32)
    up_act = jnp.dot(ffn_input, up_weight, preferred_element_type=jnp.float32)
    hidden = (jax.nn.silu(gate_act) * up_act).astype(jnp.bfloat16)
    ffn_out = grouped_sum(hidden, down_weight)
    return (resid_sum.astype(jnp.float32) + ffn_out).astype(jnp.bfloat16)
```

```python
import functools

import jax
import jax.numpy as jnp
from jax import lax
from jax.experimental import pallas as pl
from jax.experimental.pallas import tpu as pltpu
from jax.sharding import Mesh
from jax.sharding import PartitionSpec as P

HEAD_DIM = 64
Q_COLS = 512
AXES = ("x", "zh", "core", "y", "zl")
NY = 4
MESH = pl.DeviceIdType.MESH
F32 = jnp.float32
BF16 = jnp.bfloat16

UP, DOWN, ACROSS, GATHER = 0, 3, 6, 14
FAR_UP, FAR_DOWN, NEAR_UP, NEAR_DOWN, REDUCE = 4, 5, 6, 8, 10
AG1 = 0
RS1 = AG1 + GATHER
AG2 = RS1 + REDUCE
RS2 = AG2 + GATHER
SWAP = RS2 + REDUCE
BACK = SWAP + 2
SEGS = BACK + 2
WEIGHTS = SEGS + 1
SLOTS = WEIGHTS + 10


def tiles(total, step):
    return [(at, min(step, total - at)) for at in range(0, total, step)]


def norm_rows(rows, gain):
    floats = rows.astype(F32)
    mean_square = jnp.mean(floats * floats, axis=-1, keepdims=True)
    return (floats * lax.rsqrt(mean_square + 1e-05) * gain).astype(BF16)


def kernel(
    x_ref, seg_ref, again_ref, qkv_ref, out_ref, fgain_ref, gate_ref, up_ref, down_ref,
    y_ref,
    xg, rg, pa, pb, across_a, across_b, far_a, far_b, near_a, near_b,
    wq, wo, wg, wu, wd, proj, kpad, vpad, mixed, bias, normed, segs, final,
    send_sem, recv_sem, local_sem,
):
    half, width = xg.shape[1], xg.shape[2]
    chunk = 4 * half
    x, zh = lax.axis_index("x"), lax.axis_index("zh")
    core, y, zl = lax.axis_index("core"), lax.axis_index("y"), lax.axis_index("zl")
    nzh = lax.axis_size("zh")
    other = 1 - core
    pair_z = 1 - zl
    far_zh = lax.rem(zh + 2 * zl - 1 + nzh, nzh)
    wrong = lax.rem(core + zl, 2)

    def dev(zh_=zh, core_=core, y_=y, zl_=zl):
        return (x, zh_, core_, y_, zl_)

    up_dev = dev(y_=lax.rem(y + 1, NY))
    down_dev = dev(y_=lax.rem(y + NY - 1, NY))
    mate = dev(core_=other)
    pair = dev(zl_=pair_z)
    beyond = dev(zh_=far_zh, zl_=pair_z)
    partner = dev(core_=other, zl_=pair_z)

    def mine(dy):
        return 4 * lax.rem(y + dy, NY) + 2 * core

    def theirs(dy):
        return 4 * lax.rem(y + dy, NY) + 2 * other

    def copy(src, dst, slot, device):
        return pltpu.make_async_remote_copy(
            src_ref=src, dst_ref=dst, send_sem=send_sem.at[slot], recv_sem=recv_sem.at[slot],
            device_id=device, device_id_type=MESH,
        )

    def arrived(dst, slot):
        copy(dst, dst, slot, mate).wait_recv()

    def sent(src, slot):
        copy(src, src, slot, mate).wait_send()

    barrier = pltpu.get_barrier_semaphore()
    for device in (up_dev, down_dev, mate, pair, beyond):
        pl.semaphore_signal(barrier, inc=1, device_id=device, device_id_type=MESH)

    @pl.when(wrong == 1)
    def _():
        pl.semaphore_signal(barrier, inc=1, device_id=partner, device_id_type=MESH)

    pl.semaphore_wait(barrier, 5 + wrong)

    weights = [(qkv_ref, wq, 0.4), (out_ref, wo, 0.5), (gate_ref, wg, 0.5), (up_ref, wu, 0.5), (down_ref, wd, 0.5)]
    weights = [
        (src, dst, ((0, int(dst.shape[0] * part) // 16 * 16), (int(dst.shape[0] * part) // 16 * 16, dst.shape[0])))
        for src, dst, part in weights
    ]

    def weight_wait(at):
        _, dst, cuts = weights[at]

        @pl.when(wrong == 0)
        def _():
            pltpu.make_async_copy(weights[at][0], dst, local_sem.at[at]).wait()

        @pl.when(wrong == 1)
        def _():
            for side, (lo, hi) in enumerate(cuts):
                arrived(dst.at[pl.ds(lo, hi - lo)], WEIGHTS + 2 * at + side)

    own = mine(0)

    @pl.when(wrong == 0)
    def _():
        for piece in range(2):
            pltpu.make_async_copy(
                x_ref.at[pl.ds(piece * half, half)], xg.at[own + piece], local_sem.at[5 + piece]
            ).start()
        copy(seg_ref, segs, SEGS, mate).start()
        for at, (src, dst, cuts) in enumerate(weights):
            for side, (lo, hi) in enumerate(cuts):
                copy(
                    src.at[pl.ds(lo, hi - lo)], dst.at[pl.ds(lo, hi - lo)],
                    WEIGHTS + 2 * at + side, (pair, beyond)[side],
                ).start()
        for at, (src, dst, cuts) in enumerate(weights):
            pltpu.make_async_copy(src, dst, local_sem.at[at]).start()
        segs[...] = seg_ref[...]

    @pl.when(wrong == 1)
    def _():
        for piece in range(2):
            copy(
                x_ref.at[pl.ds(piece * half, half)], xg.at[theirs(0) + piece], SWAP + piece, partner
            ).start()

    def up_send(buf, base, slot, piece):
        copy(buf.at[piece], buf.at[piece], base + UP + slot, up_dev).start()

    def down_send(buf, base, slot, piece):
        copy(buf.at[piece], buf.at[piece], base + DOWN + slot, down_dev).start()

    def cross(buf, base, dy, piece):
        at = mine(dy) + piece
        copy(buf.at[at], buf.at[at], base + ACROSS + 2 * dy + piece, mate).start()

    def crossed(buf, base, dy):
        for piece in range(2):
            arrived(buf.at[theirs(dy) + piece], base + ACROSS + 2 * dy + piece)

    def gather_start(buf, base, ready):
        ready(0)
        up_send(buf, base, 0, own)
        cross(buf, base, 0, 0)
        ready(1)
        down_send(buf, base, 0, own + 1)
        cross(buf, base, 0, 1)
        up_send(buf, base, 1, own + 1)
        down_send(buf, base, 1, own)

    def gather_forward(buf, base):
        arrived(buf.at[mine(3)], base + UP)
        up_send(buf, base, 2, mine(3))
        cross(buf, base, 3, 0)
        arrived(buf.at[mine(1) + 1], base + DOWN)
        down_send(buf, base, 2, mine(1) + 1)
        cross(buf, base, 1, 1)

    def gather_near(buf, base):
        arrived(buf.at[mine(3) + 1], base + UP + 1)
        cross(buf, base, 3, 1)
        arrived(buf.at[mine(1)], base + DOWN + 1)
        cross(buf, base, 1, 0)

    def gather_far(buf, base):
        arrived(buf.at[mine(2)], base + UP + 2)
        cross(buf, base, 2, 0)
        arrived(buf.at[mine(2) + 1], base + DOWN + 2)
        cross(buf, base, 2, 1)

    def gather_sent(buf, base):
        piece = buf.at[own]
        for slot in range(GATHER):
            sent(piece, base + slot)

    def exchange(part, acc, base, dy):
        copy(part.at[pl.ds(theirs(dy), 2)], acc.at[dy], base + dy, mate).start()

    def met(part, acc, base, dy, piece):
        at = mine(dy) + piece
        return part[at].astype(F32) + acc[dy, piece].astype(F32)

    def reduce_far(part, acc, far, base):
        arrived(acc.at[2], base + 2)
        for piece in range(2):
            part[mine(2) + piece] = met(part, acc, base, 2, piece).astype(BF16)
            copy(
                part.at[mine(2) + piece], far.at[piece], base + FAR_UP + piece, (up_dev, down_dev)[piece]
            ).start()

    def reduce_near(part, acc, far, near, base, dy, late):
        upward = dy == 1
        piece = (0 if upward else 1) if late else (1 if upward else 0)
        at = mine(dy) + piece
        if late:
            arrived(far.at[piece], base + FAR_UP + piece)
            part[at] = (met(part, acc, base, dy, piece) + far[piece].astype(F32)).astype(BF16)
        else:
            arrived(acc.at[dy], base + dy)
            part[at] = met(part, acc, base, dy, piece).astype(BF16)
        side = 0 if upward else 1
        copy(
            part.at[at], near.at[side, piece], base + (NEAR_UP, NEAR_DOWN)[side] + piece, (up_dev, down_dev)[side]
        ).start()

    def reduce_own(part, acc, near, base, piece):
        arrived(near.at[0, piece], base + NEAR_UP + piece)
        arrived(near.at[1, piece], base + NEAR_DOWN + piece)
        return met(part, acc, base, 0, piece) + (near[0, piece].astype(F32) + near[1, piece].astype(F32))

    def reduce_sent(part, acc, far, near, base):
        for dy in range(4):
            sent(acc.at[dy], base + dy)
        for slot in range(FAR_UP, REDUCE):
            sent(far.at[0], base + slot)

    def own_ready(piece):
        @pl.when(wrong == 0)
        def _():
            pltpu.make_async_copy(
                x_ref.at[pl.ds(piece * half, half)], xg.at[own + piece], local_sem.at[5 + piece]
            ).wait()

        @pl.when(wrong == 1)
        def _():
            arrived(xg.at[own + piece], SWAP + piece)

    gather_start(xg, AG1, own_ready)
    gather_forward(xg, AG1)
    gather_near(xg, AG1)
    gather_far(xg, AG1)

    @pl.when(wrong == 1)
    def _():
        arrived(segs, SEGS)

    weight_wait(0)
    for dy in range(4):
        crossed(xg, AG1, dy)
    zeros = jnp.zeros((chunk, HEAD_DIM), BF16)

    def project(u, carry):
        rows = pl.ds(pl.multiple_of(u * chunk, chunk), chunk)
        normed[...] = norm_rows(xg[pl.ds(4 * u, 4)].reshape(chunk, width), again_ref[...])
        result = jnp.dot(normed[...], wq[...], preferred_element_type=F32).astype(BF16)
        proj[rows, :] = result[:, :Q_COLS]
        keys = result[:, Q_COLS : Q_COLS + HEAD_DIM]
        values = result[:, Q_COLS + HEAD_DIM :]
        kpad[0, rows, :] = jnp.concatenate([keys, zeros], axis=1)
        kpad[1, rows, :] = jnp.concatenate([zeros, keys], axis=1)
        vpad[0, rows, :] = jnp.concatenate([values, zeros], axis=1)
        vpad[1, rows, :] = jnp.concatenate([zeros, values], axis=1)
        return carry

    lax.fori_loop(0, NY, project, 0)

    def attend(at):
        seen = (at + 1) * chunk
        rows = pl.ds(at * chunk, chunk)
        query_seg = jnp.broadcast_to(segs[:, at * chunk : seen], (128, chunk)).T[:, :1]
        query_pos = at * chunk + lax.broadcasted_iota(jnp.int32, (chunk, seen), 0)
        key_pos = lax.broadcasted_iota(jnp.int32, (chunk, seen), 1)
        allowed = (key_pos <= query_pos) & (segs[:, :seen] == query_seg)
        bias[:, :seen] = jnp.where(allowed, 0.0, -1e30)
        lane = lax.broadcasted_iota(jnp.int32, (chunk, 128), 1)

        def heads(j, carry):
            cols = pl.ds(pl.multiple_of(j * 128, 128), 128)
            query = proj[rows, cols]
            total, norm = None, []
            for side in range(2):
                scores = lax.dot_general(
                    query, kpad[side, :seen, :], (((1,), (1,)), ((), ())), preferred_element_type=F32
                )
                scores = scores * HEAD_DIM ** (-0.5) + bias[:, :seen]
                weight = jnp.exp(scores - jnp.max(scores, axis=-1, keepdims=True))
                norm.append(jnp.sum(weight, axis=-1, keepdims=True))
                value = jnp.dot(weight.astype(BF16), vpad[side, :seen, :], preferred_element_type=F32)
                total = value if total is None else total + value
            mixed[:, cols] = (total / jnp.where(lane < HEAD_DIM, norm[0], norm[1])).astype(BF16)
            return carry

        lax.fori_loop(0, Q_COLS // 128, heads, 0)

    weight_wait(1)

    def attention_step(i, carry):
        dy = lax.rem(2 + i + (i // 2) * (1 - 2 * lax.rem(i, 2)), NY)
        u = lax.rem(y + dy, NY)
        for at in range(NY):
            @pl.when(u == at)
            def _():
                attend(at)
        for lo, size in tiles(width, 640):
            part = jnp.dot(mixed[...], wo[:, lo : lo + size], preferred_element_type=F32)
            pa[pl.ds(4 * u, 4), :, lo : lo + size] = part.astype(BF16).reshape(4, half, size)
        exchange(pa, across_a, RS1, dy)

        @pl.when(i == 1)
        def _():
            reduce_far(pa, across_a, far_a, RS1)

        @pl.when(i == 2)
        def _():
            reduce_near(pa, across_a, far_a, near_a, RS1, 3, False)

        @pl.when(i == 3)
        def _():
            reduce_near(pa, across_a, far_a, near_a, RS1, 1, False)

        return carry

    lax.fori_loop(0, NY, attention_step, 0)
    reduce_near(pa, across_a, far_a, near_a, RS1, 3, True)
    reduce_near(pa, across_a, far_a, near_a, RS1, 1, True)
    arrived(across_a.at[0], RS1)

    def resid_ready(piece):
        total = reduce_own(pa, across_a, near_a, RS1, piece)
        rg[own + piece] = (xg[own + piece].astype(F32) + total).astype(BF16)

    gather_start(rg, AG2, resid_ready)
    gather_forward(rg, AG2)
    for at in (2, 3, 4):
        weight_wait(at)

    def ffn_step(i, carry):
        dy = lax.rem(3 * i + (i // 2) * (3 + 2 * lax.rem(i, 2)), NY)
        u = lax.rem(y + dy, NY)

        @pl.when(i == 1)
        def _():
            gather_near(rg, AG2)

        @pl.when(i == 3)
        def _():
            gather_far(rg, AG2)

        for piece in range(2):
            arrived(rg.at[theirs(dy) + piece], AG2 + ACROSS + 2 * dy + piece)
        normed[...] = norm_rows(rg[pl.ds(4 * u, 4)].reshape(chunk, width), fgain_ref[...])
        gate = jnp.dot(normed[...], wg[...], preferred_element_type=F32)
        lift = jnp.dot(normed[...], wu[...], preferred_element_type=F32)
        hidden = (gate / (1.0 + jnp.exp(-gate)) * lift).astype(BF16)
        for lo, size in tiles(width, 640):
            part = jnp.dot(hidden, wd[:, lo : lo + size], preferred_element_type=F32)
            pb[pl.ds(4 * u, 4), :, lo : lo + size] = part.astype(BF16).reshape(4, half, size)
        exchange(pb, across_b, RS2, dy)

        @pl.when(i == 2)
        def _():
            reduce_near(pb, across_b, far_b, near_b, RS2, 3, False)

        @pl.when(i == 3)
        def _():
            reduce_near(pb, across_b, far_b, near_b, RS2, 1, False)

        return carry

    lax.fori_loop(0, NY, ffn_step, 0)
    reduce_far(pb, across_b, far_b, RS2)
    reduce_near(pb, across_b, far_b, near_b, RS2, 3, True)
    reduce_near(pb, across_b, far_b, near_b, RS2, 1, True)
    arrived(across_b.at[0], RS2)
    for piece in range(2):
        total = reduce_own(pb, across_b, near_b, RS2, piece)
        final[piece] = (rg[own + piece].astype(F32) + total).astype(BF16)
        place = y_ref.at[pl.ds(piece * half, half)]

        @pl.when(wrong == 0)
        def _():
            pltpu.make_async_copy(final.at[piece], place, local_sem.at[7 + piece]).start()

        @pl.when(wrong == 1)
        def _():
            copy(final.at[piece], place, BACK + piece, partner).start()

    gather_sent(xg, AG1)
    gather_sent(rg, AG2)
    reduce_sent(pa, across_a, far_a, near_a, RS1)
    reduce_sent(pb, across_b, far_b, near_b, RS2)

    @pl.when(wrong == 0)
    def _():
        sent(segs, SEGS)
        for at, (src, dst, cuts) in enumerate(weights):
            for side, (lo, hi) in enumerate(cuts):
                sent(dst.at[pl.ds(lo, hi - lo)], WEIGHTS + 2 * at + side)
        for piece in range(2):
            pltpu.make_async_copy(
                final.at[piece], y_ref.at[pl.ds(piece * half, half)], local_sem.at[7 + piece]
            ).wait()

    @pl.when(wrong == 1)
    def _():
        for piece in range(2):
            place = y_ref.at[pl.ds(piece * half, half)]
            sent(xg.at[own], SWAP + piece)
            sent(final.at[piece], BACK + piece)
            arrived(place, BACK + piece)


def shards(
    activations, segment_ids, attn_gain, qkv_weight, out_weight, ffn_gain, gate_weight, up_weight, down_weight
):
    rows, width = activations.shape
    half, tokens = rows // 2, rows * 8
    chunk = 2 * rows
    vmem = pltpu.VMEM
    whole = pl.BlockSpec(memory_space=pltpu.VMEM)
    away = pl.BlockSpec(memory_space=pl.ANY)
    return pl.pallas_call(
        kernel,
        out_shape=jax.ShapeDtypeStruct((rows, width), BF16),
        in_specs=[away, whole, whole, away, away, whole, away, away, away],
        out_specs=away,
        scratch_shapes=[
            vmem((16, half, width), BF16),
            vmem((16, half, width), BF16),
            vmem((16, half, width), BF16),
            vmem((16, half, width), BF16),
            vmem((4, 2, half, width), BF16),
            vmem((4, 2, half, width), BF16),
            vmem((2, half, width), BF16),
            vmem((2, half, width), BF16),
            vmem((2, 2, half, width), BF16),
            vmem((2, 2, half, width), BF16),
            vmem(qkv_weight.shape, BF16),
            vmem(out_weight.shape, BF16),
            vmem(gate_weight.shape, BF16),
            vmem(up_weight.shape, BF16),
            vmem(down_weight.shape, BF16),
            vmem((tokens, Q_COLS), BF16),
            vmem((2, tokens, 128), BF16),
            vmem((2, tokens, 128), BF16),
            vmem((chunk, Q_COLS), BF16),
            vmem((chunk, tokens), F32),
            vmem((chunk, width), BF16),
            vmem((1, tokens), jnp.int32),
            vmem((2, half, width), BF16),
            pltpu.SemaphoreType.DMA((SLOTS,)),
            pltpu.SemaphoreType.DMA((SLOTS,)),
            pltpu.SemaphoreType.DMA((9,)),
        ],
        compiler_params=pltpu.CompilerParams(
            collective_id=0, has_side_effects=True, vmem_limit_bytes=67043328
        ),
    )(
        activations, segment_ids.reshape(1, tokens), attn_gain.reshape(1, width), qkv_weight, out_weight,
        ffn_gain.reshape(1, width), gate_weight, up_weight, down_weight,
    )


def solution(mesh):
    groups = mesh.shape["dp"] // 8
    torus = Mesh(mesh.devices.reshape(4, groups, 2, NY, 2), AXES)
    dp, tensor = ("x", "zh", "core"), ("y", "zl")
    in_specs = (
        P(dp + tensor, None), P(dp), P(), P(None, tensor), P(tensor, None), P(),
        P(None, tensor), P(None, tensor), P(tensor, None),
    )
    return jax.shard_map(
        shards, mesh=torus, in_specs=in_specs, out_specs=P(dp + tensor, None), check_vma=False
    )
```

```python
import functools

import jax
import jax.numpy as jnp
from jax import lax
from jax.experimental import pallas as pl
from jax.experimental.pallas import tpu as pltpu
from jax.sharding import Mesh
from jax.sharding import PartitionSpec as P

HEAD_DIM = 64
Q_COLS = 512
AXES = ("x", "zh", "core", "y", "zl")
NY = 4
MESH = pl.DeviceIdType.MESH
F32 = jnp.float32
BF16 = jnp.bfloat16

UP, DOWN, ACROSS, GATHER = 0, 3, 6, 14
FAR, NEAR_UP, NEAR_DOWN, REDUCE = 4, 6, 8, 10
AG1 = 0
RS1 = AG1 + 2 * GATHER
AG2 = RS1 + 2 * REDUCE
RS2 = AG2 + 2 * GATHER
SWAP = RS2 + 2 * REDUCE
BACK = SWAP + 2
SEGS = BACK + 2
WEIGHTS = SEGS + 1
SLOTS = WEIGHTS + 10


def tiles(total, step):
    return [(at, min(step, total - at)) for at in range(0, total, step)]


def dot_t(left, right):
    return lax.dot_general(left, right, (((1,), (1,)), ((), ())), preferred_element_type=F32)


def norm_rows(rows, gain):
    floats = rows.astype(F32)
    mean_square = jnp.mean(floats * floats, axis=-1, keepdims=True)
    return (floats * lax.rsqrt(mean_square + 1e-05) * gain).astype(BF16)


def kernel(
    x_ref, seg_ref, again_ref, qkv_ref, out_ref, fgain_ref, gate_ref, up_ref, down_ref,
    y_ref,
    xg, rg, pa, pb, across_a, across_b, far_a, far_b, near_a, near_b,
    wq, wo, wg, wu, wd, queries, kpad, vpad, mixed, bias, normed, segs, final,
    send_sem, recv_sem, local_sem,
):
    half, width = xg.shape[1], xg.shape[2]
    chunk = 4 * half
    x, zh = lax.axis_index("x"), lax.axis_index("zh")
    core, y, zl = lax.axis_index("core"), lax.axis_index("y"), lax.axis_index("zl")
    nzh = lax.axis_size("zh")
    other = 1 - core
    pair_z = 1 - zl
    far_zh = lax.rem(zh + 2 * zl - 1 + nzh, nzh)
    wrong = lax.rem(core + zl, 2)

    def dev(zh_=zh, core_=core, y_=y, zl_=zl):
        return (x, zh_, core_, y_, zl_)

    up_dev = dev(y_=lax.rem(y + 1, NY))
    down_dev = dev(y_=lax.rem(y + NY - 1, NY))
    mate = dev(core_=other)
    beyond = dev(zh_=far_zh, zl_=pair_z)
    partner = dev(core_=other, zl_=pair_z)

    def mine(dy):
        return 4 * lax.rem(y + dy, NY) + 2 * core

    def theirs(dy):
        return 4 * lax.rem(y + dy, NY) + 2 * other

    def copy(src, dst, slot, device):
        return pltpu.make_async_remote_copy(
            src_ref=src, dst_ref=dst, send_sem=send_sem.at[slot], recv_sem=recv_sem.at[slot],
            device_id=device, device_id_type=MESH,
        )

    def arrived(dst, slot):
        copy(dst, dst, slot, mate).wait_recv()

    def sent(src, slot):
        copy(src, src, slot, mate).wait_send()

    barrier = pltpu.get_barrier_semaphore()
    for device in (up_dev, down_dev, mate, beyond):
        pl.semaphore_signal(barrier, inc=1, device_id=device, device_id_type=MESH)

    @pl.when(wrong == 1)
    def _():
        pl.semaphore_signal(barrier, inc=1, device_id=partner, device_id_type=MESH)

    pl.semaphore_wait(barrier, 4 + wrong)

    weights = [(qkv_ref, wq, 0.4), (out_ref, wo, 0.5), (gate_ref, wg, 0.5), (up_ref, wu, 0.5), (down_ref, wd, 0.5)]
    weights = [
        (src, dst, ((0, int(dst.shape[0] * part) // 16 * 16), (int(dst.shape[0] * part) // 16 * 16, dst.shape[0])))
        for src, dst, part in weights
    ]

    def weight_wait(at):
        _, dst, cuts = weights[at]

        @pl.when(wrong == 0)
        def _():
            pltpu.make_async_copy(weights[at][0], dst, local_sem.at[at]).wait()

        @pl.when(wrong == 1)
        def _():
            for side, (lo, hi) in enumerate(cuts):
                arrived(dst.at[pl.ds(lo, hi - lo)], WEIGHTS + 2 * at + side)

    def send_weights(side, device):
        for at, (src, dst, cuts) in enumerate(weights):
            lo, hi = cuts[side]
            copy(src.at[pl.ds(lo, hi - lo)], dst.at[pl.ds(lo, hi - lo)], WEIGHTS + 2 * at + side, device).start()

    def weights_sent(side):
        for at, (src, dst, cuts) in enumerate(weights):
            lo, hi = cuts[side]
            sent(dst.at[pl.ds(lo, hi - lo)], WEIGHTS + 2 * at + side)

    own = mine(0)

    @pl.when(wrong == 0)
    def _():
        for piece in range(2):
            pltpu.make_async_copy(
                x_ref.at[pl.ds(piece * half, half)], xg.at[own + piece], local_sem.at[5 + piece]
            ).start()
        copy(seg_ref, segs, SEGS, mate).start()
        send_weights(1, beyond)
        for at, (src, dst, cuts) in enumerate(weights):
            pltpu.make_async_copy(src, dst, local_sem.at[at]).start()
        segs[...] = seg_ref[...]

    @pl.when(wrong == 1)
    def _():
        for piece in range(2):
            copy(
                x_ref.at[pl.ds(piece * half, half)], xg.at[theirs(0) + piece], SWAP + piece, partner
            ).start()
        send_weights(0, partner)

    cut = width // 256 * 128
    runs = (pl.ds(0, cut), pl.ds(cut, width - cut))

    def run_of(buf, at, side):
        return buf.at[at, :, runs[side]]

    def spread(buf, base, at, side, slot, device):
        piece = run_of(buf, at, side)
        copy(piece, piece, base + slot, device).start()

    def cross(buf, base, p, dy, side):
        spread(buf, base, mine(dy) + p, side, ACROSS + 2 * dy + side, mate)

    def crossed(buf, base, dy, p):
        base = base + p * GATHER
        for side in range(2):
            arrived(run_of(buf, theirs(dy) + p, side), base + ACROSS + 2 * dy + side)

    def gather_start(buf, base, p):
        base = base + p * GATHER
        spread(buf, base, own + p, 0, UP, up_dev)
        spread(buf, base, own + p, 1, DOWN, down_dev)
        cross(buf, base, p, 0, 0)
        cross(buf, base, p, 0, 1)
        spread(buf, base, own + p, 1, UP + 1, up_dev)
        spread(buf, base, own + p, 0, DOWN + 1, down_dev)

    def gather_forward(buf, base, p):
        base = base + p * GATHER
        arrived(run_of(buf, mine(3) + p, 0), base + UP)
        spread(buf, base, mine(3) + p, 0, UP + 2, up_dev)
        cross(buf, base, p, 3, 0)
        arrived(run_of(buf, mine(1) + p, 1), base + DOWN)
        spread(buf, base, mine(1) + p, 1, DOWN + 2, down_dev)
        cross(buf, base, p, 1, 1)

    def gather_near(buf, base, p):
        base = base + p * GATHER
        arrived(run_of(buf, mine(3) + p, 1), base + UP + 1)
        cross(buf, base, p, 3, 1)
        arrived(run_of(buf, mine(1) + p, 0), base + DOWN + 1)
        cross(buf, base, p, 1, 0)

    def gather_far(buf, base, p):
        base = base + p * GATHER
        arrived(run_of(buf, mine(2) + p, 0), base + UP + 2)
        cross(buf, base, p, 2, 0)
        arrived(run_of(buf, mine(2) + p, 1), base + DOWN + 2)
        cross(buf, base, p, 2, 1)

    def gather_sent(buf, base):
        for p in range(2):
            for dy in range(4):
                for side in range(2):
                    sent(run_of(buf, own, side), base + p * GATHER + ACROSS + 2 * dy + side)
            for slot, side in ((UP, 0), (UP + 1, 1), (UP + 2, 0), (DOWN, 1), (DOWN + 1, 0), (DOWN + 2, 1)):
                sent(run_of(buf, own, side), base + p * GATHER + slot)

    def exchange(part, acc, base, p, dy):
        copy(part.at[theirs(dy) + p], acc.at[dy, p], base + p * REDUCE + dy, mate).start()

    def met(part, acc, p, dy, cols):
        return part[mine(dy) + p, :, cols].astype(F32) + acc[dy, p, :, cols].astype(F32)

    def reduce_far(part, acc, far, base, p):
        base = base + p * REDUCE
        arrived(acc.at[2, p], base + 2)
        for side, cols in enumerate(runs):
            at = mine(2) + p
            part[at, :, cols] = met(part, acc, p, 2, cols).astype(BF16)
            copy(
                run_of(part, at, side), run_of(far, p, side), base + FAR + side, (up_dev, down_dev)[side]
            ).start()

    def reduce_near(part, acc, far, near, base, p, dy, late):
        base = base + p * REDUCE
        way = 0 if dy == 1 else 1
        side = way if late else 1 - way
        at, cols = mine(dy) + p, runs[side]
        if late:
            arrived(run_of(far, p, side), base + FAR + side)
            part[at, :, cols] = (met(part, acc, p, dy, cols) + far[p, :, cols].astype(F32)).astype(BF16)
        else:
            arrived(acc.at[dy, p], base + dy)
            part[at, :, cols] = met(part, acc, p, dy, cols).astype(BF16)
        copy(
            run_of(part, at, side), near.at[way, p, :, cols], base + (NEAR_UP, NEAR_DOWN)[way] + side,
            (up_dev, down_dev)[way],
        ).start()

    def reduce_own(part, acc, near, base, p, first, result):
        base = base + p * REDUCE
        arrived(acc.at[0, p], base)
        for side, cols in enumerate(runs):
            for way in range(2):
                arrived(near.at[way, p, :, cols], base + (NEAR_UP, NEAR_DOWN)[way] + side)
            total = met(part, acc, p, 0, cols) + (
                near[0, p, :, cols].astype(F32) + near[1, p, :, cols].astype(F32)
            )
            at = own + p
            result(cols, (first[at, :, cols].astype(F32) + total).astype(BF16))

    def reduce_sent(part, acc, base):
        for p in range(2):
            for dy in range(4):
                sent(acc.at[dy, p], base + p * REDUCE + dy)
            for slot in (FAR, NEAR_UP, NEAR_DOWN):
                for side in range(2):
                    sent(run_of(part, own, side), base + p * REDUCE + slot + side)

    def own_ready(piece):
        @pl.when(wrong == 0)
        def _():
            pltpu.make_async_copy(
                x_ref.at[pl.ds(piece * half, half)], xg.at[own + piece], local_sem.at[5 + piece]
            ).wait()

        @pl.when(wrong == 1)
        def _():
            arrived(xg.at[own + piece], SWAP + piece)

    for p in range(2):
        own_ready(p)
        gather_start(xg, AG1, p)
    for p in range(2):
        gather_forward(xg, AG1, p)
    for p in range(2):
        gather_near(xg, AG1, p)

    @pl.when(wrong == 1)
    def _():
        arrived(segs, SEGS)

    weight_wait(0)
    zeros = jnp.zeros((chunk, HEAD_DIM), BF16)

    def arrival(i):
        return lax.rem(3 * i + (i // 2) * (3 + 2 * lax.rem(i, 2)), NY)

    def project(i, carry):
        dy = arrival(i)
        u = lax.rem(y + dy, NY)

        @pl.when(i == 3)
        def _():
            gather_far(xg, AG1, 0)
            gather_far(xg, AG1, 1)

        crossed(xg, AG1, dy, 0)
        crossed(xg, AG1, dy, 1)
        rows = pl.ds(pl.multiple_of(u * chunk, chunk), chunk)
        normed[...] = norm_rows(xg[pl.ds(4 * u, 4)].reshape(chunk, width), again_ref[...])
        result = jnp.dot(normed[...], wq[...], preferred_element_type=F32).astype(BF16)
        for piece in range(4):
            queries[piece % 2, u, piece // 2] = result[piece * half : (piece + 1) * half, :Q_COLS]
        keys = result[:, Q_COLS : Q_COLS + HEAD_DIM]
        values = result[:, Q_COLS + HEAD_DIM :]
        kpad[0, rows, :] = jnp.concatenate([keys, zeros], axis=1)
        kpad[1, rows, :] = jnp.concatenate([zeros, keys], axis=1)
        vpad[0, rows, :] = jnp.concatenate([values, zeros], axis=1)
        vpad[1, rows, :] = jnp.concatenate([zeros, values], axis=1)
        return carry

    lax.fori_loop(0, NY, project, 0)

    rows_now = 2 * half

    def attend(at, p):
        seen = (at + 1) * chunk
        query_seg = jnp.broadcast_to(segs[:, at * chunk : seen], (128, chunk)).T[:, :1]
        query_seg = jnp.concatenate(
            [query_seg[(2 * c + p) * half : (2 * c + p + 1) * half] for c in range(2)], axis=0
        )
        row = lax.broadcasted_iota(jnp.int32, (rows_now, seen), 0)
        query_pos = at * chunk + p * half + row + jnp.where(row >= half, half, 0)
        key_pos = lax.broadcasted_iota(jnp.int32, (rows_now, seen), 1)
        allowed = (key_pos <= query_pos) & (segs[:, :seen] == query_seg)
        bias[:, :seen] = jnp.where(allowed, 0.0, -1e30)
        lane = lax.broadcasted_iota(jnp.int32, (rows_now, 128), 1)

        def heads(j, carry):
            cols = pl.ds(pl.multiple_of(j * 128, 128), 128)
            query = queries[p, at, :, :, cols].reshape(rows_now, 128)
            total, norm = None, []
            for side in range(2):
                scores = dot_t(query, kpad[side, :seen, :])
                scores = scores * HEAD_DIM ** (-0.5) + bias[:, :seen]
                weight = jnp.exp(scores - jnp.max(scores, axis=-1, keepdims=True))
                norm.append(jnp.sum(weight, axis=-1, keepdims=True))
                value = jnp.dot(weight.astype(BF16), vpad[side, :seen, :], preferred_element_type=F32)
                total = value if total is None else total + value
            mixed[:, cols] = (total / jnp.where(lane < HEAD_DIM, norm[0], norm[1])).astype(BF16)
            return carry

        lax.fori_loop(0, Q_COLS // 128, heads, 0)

    def put(part, u, p, left, right):
        for lo, size in tiles(width, 640):
            block = dot_t(left, right[lo : lo + size, :]).astype(BF16)
            for c in range(2):
                part[4 * u + 2 * c + p, :, lo : lo + size] = block[c * half : (c + 1) * half]

    def attention_step(p, i, carry):
        dy = lax.rem(2 + i + (i // 2) * (1 - 2 * lax.rem(i, 2)), NY)
        u = lax.rem(y + dy, NY)
        for at in range(NY):
            @pl.when(u == at)
            def _():
                attend(at, p)

        if p == 0:
            @pl.when(i == 0)
            def _():
                weight_wait(1)

        put(pa, u, p, mixed[...], wo)
        exchange(pa, across_a, RS1, p, dy)
        if p == 1:
            @pl.when(i == 0)
            def _():
                reduce_near(pa, across_a, far_a, near_a, RS1, 0, 3, True)
                reduce_near(pa, across_a, far_a, near_a, RS1, 0, 1, True)

        @pl.when(i == 1)
        def _():
            reduce_far(pa, across_a, far_a, RS1, p)

        @pl.when(i == 2)
        def _():
            reduce_near(pa, across_a, far_a, near_a, RS1, p, 3, False)

        @pl.when(i == 3)
        def _():
            reduce_near(pa, across_a, far_a, near_a, RS1, p, 1, False)

        return carry

    lax.fori_loop(0, NY, functools.partial(attention_step, 0), 0)
    lax.fori_loop(0, NY, functools.partial(attention_step, 1), 0)

    def resid_ready(p):
        def result(cols, value):
            rg[own + p, :, cols] = value

        reduce_own(pa, across_a, near_a, RS1, p, xg, result)

    resid_ready(0)
    gather_start(rg, AG2, 0)
    reduce_near(pa, across_a, far_a, near_a, RS1, 1, 3, True)
    reduce_near(pa, across_a, far_a, near_a, RS1, 1, 1, True)
    gather_forward(rg, AG2, 0)
    resid_ready(1)
    gather_start(rg, AG2, 1)
    for at in (2, 3, 4):
        weight_wait(at)

    def ffn_step(p, i, carry):
        dy = arrival(i)
        u = lax.rem(y + dy, NY)

        @pl.when(i == 1)
        def _():
            gather_near(rg, AG2, p)
            if p == 0:
                gather_forward(rg, AG2, 1)

        @pl.when(i == 3)
        def _():
            gather_far(rg, AG2, p)

        crossed(rg, AG2, dy, p)
        rows_in = jnp.concatenate([rg[4 * u + p], rg[4 * u + 2 + p]], axis=0)
        normed[:rows_now, :] = norm_rows(rows_in, fgain_ref[...])
        rows_in = normed[:rows_now, :]
        gate = jnp.dot(rows_in, wg[...], preferred_element_type=F32)
        lift = jnp.dot(rows_in, wu[...], preferred_element_type=F32)
        hidden = (gate / (1.0 + jnp.exp(-gate)) * lift).astype(BF16)
        put(pb, u, p, hidden, wd)
        exchange(pb, across_b, RS2, p, dy)
        if p == 1:
            @pl.when(i == 0)
            def _():
                reduce_far(pb, across_b, far_b, RS2, 0)

        @pl.when(i == 2)
        def _():
            reduce_near(pb, across_b, far_b, near_b, RS2, p, 3, False)
            if p == 1:
                reduce_near(pb, across_b, far_b, near_b, RS2, 0, 3, True)
                reduce_near(pb, across_b, far_b, near_b, RS2, 0, 1, True)

        @pl.when(i == 3)
        def _():
            reduce_near(pb, across_b, far_b, near_b, RS2, p, 1, False)

        return carry

    lax.fori_loop(0, NY, functools.partial(ffn_step, 0), 0)
    lax.fori_loop(0, NY, functools.partial(ffn_step, 1), 0)

    def finish(p):
        def result(cols, value):
            final[p, :, cols] = value

        reduce_own(pb, across_b, near_b, RS2, p, rg, result)
        place = y_ref.at[pl.ds(p * half, half)]

        @pl.when(wrong == 0)
        def _():
            pltpu.make_async_copy(final.at[p], place, local_sem.at[7 + p]).start()

        @pl.when(wrong == 1)
        def _():
            copy(final.at[p], place, BACK + p, partner).start()

    reduce_far(pb, across_b, far_b, RS2, 1)
    finish(0)
    reduce_near(pb, across_b, far_b, near_b, RS2, 1, 3, True)
    reduce_near(pb, across_b, far_b, near_b, RS2, 1, 1, True)
    finish(1)

    gather_sent(xg, AG1)
    gather_sent(rg, AG2)
    reduce_sent(pa, across_a, RS1)
    reduce_sent(pb, across_b, RS2)

    @pl.when(wrong == 0)
    def _():
        sent(segs, SEGS)
        weights_sent(1)
        for piece in range(2):
            pltpu.make_async_copy(
                final.at[piece], y_ref.at[pl.ds(piece * half, half)], local_sem.at[7 + piece]
            ).wait()

    @pl.when(wrong == 1)
    def _():
        weights_sent(0)
        for piece in range(2):
            place = y_ref.at[pl.ds(piece * half, half)]
            sent(xg.at[own], SWAP + piece)
            sent(final.at[piece], BACK + piece)
            arrived(place, BACK + piece)


def shards(
    activations, segment_ids, attn_gain, qkv_weight, out_weight, ffn_gain, gate_weight, up_weight, down_weight
):
    rows, width = activations.shape
    half, tokens = rows // 2, rows * 8
    chunk = 2 * rows
    vmem = pltpu.VMEM
    whole = pl.BlockSpec(memory_space=pltpu.VMEM)
    away = pl.BlockSpec(memory_space=pl.ANY)
    return pl.pallas_call(
        kernel,
        out_shape=jax.ShapeDtypeStruct((rows, width), BF16),
        in_specs=[away, whole, whole, away, away, whole, away, away, away],
        out_specs=away,
        scratch_shapes=[
            vmem((16, half, width), BF16),
            vmem((16, half, width), BF16),
            vmem((16, half, width), BF16),
            vmem((16, half, width), BF16),
            vmem((4, 2, half, width), BF16),
            vmem((4, 2, half, width), BF16),
            vmem((2, half, width), BF16),
            vmem((2, half, width), BF16),
            vmem((2, 2, half, width), BF16),
            vmem((2, 2, half, width), BF16),
            vmem(qkv_weight.shape, BF16),
            vmem(out_weight.shape[::-1], BF16),
            vmem(gate_weight.shape, BF16),
            vmem(up_weight.shape, BF16),
            vmem(down_weight.shape[::-1], BF16),
            vmem((2, NY, 2, half, Q_COLS), BF16),
            vmem((2, tokens, 128), BF16),
            vmem((2, tokens, 128), BF16),
            vmem((rows, Q_COLS), BF16),
            vmem((rows, tokens), F32),
            vmem((chunk, width), BF16),
            vmem((1, tokens), jnp.int32),
            vmem((2, half, width), BF16),
            pltpu.SemaphoreType.DMA((SLOTS,)),
            pltpu.SemaphoreType.DMA((SLOTS,)),
            pltpu.SemaphoreType.DMA((9,)),
        ],
        compiler_params=pltpu.CompilerParams(
            collective_id=0, has_side_effects=True, vmem_limit_bytes=67043328
        ),
    )(
        activations, segment_ids.reshape(1, tokens), attn_gain, qkv_weight, out_weight.T,
        ffn_gain, gate_weight, up_weight, down_weight.T,
    )


def solution(mesh):
    groups = mesh.shape["dp"] // 8
    torus = Mesh(mesh.devices.reshape(4, groups, 2, NY, 2), AXES)
    dp, tensor = ("x", "zh", "core"), ("y", "zl")
    in_specs = (
        P(dp + tensor, None), P(dp), P(), P(None, tensor), P(tensor, None), P(),
        P(None, tensor), P(None, tensor), P(tensor, None),
    )
    return jax.shard_map(
        shards, mesh=torus, in_specs=in_specs, out_specs=P(dp + tensor, None), check_vma=False
    )
```

```python
import functools

import jax
import jax.numpy as jnp
from jax import lax
from jax.experimental import pallas as pl
from jax.experimental.pallas import tpu as pltpu
from jax.sharding import Mesh
from jax.sharding import PartitionSpec as P

HEAD_DIM = 64
Q_COLS = 512
AXES = ("x", "zh", "core", "y", "zl")
NY = 4
MESH = pl.DeviceIdType.MESH
F32 = jnp.float32
BF16 = jnp.bfloat16

UP, DOWN, ACROSS, GATHER = 0, 3, 6, 14
FAR, NEAR_UP, NEAR_DOWN, REDUCE = 4, 6, 8, 10
AG1 = 0
RS1 = AG1 + 2 * GATHER
AG2 = RS1 + 2 * REDUCE
RS2 = AG2 + 2 * GATHER
SWAP = RS2 + 2 * REDUCE
BACK = SWAP + 4
SEGS = BACK + 2
NEAR_Z = SEGS + 1
PIECES = ((6, 4), (6, 3), (2, 1), (2, 1), (2, 1))
BEFORE = (0, 6, 12, 14, 16)
OVER_X = NEAR_Z + 18
SLOTS = OVER_X + 18


def tiles(total, step):
    return [(at, min(step, total - at)) for at in range(0, total, step)]


def dot_t(left, right):
    return lax.dot_general(left, right, (((1,), (1,)), ((), ())), preferred_element_type=F32)


def norm_rows(rows, gain):
    floats = rows.astype(F32)
    mean_square = jnp.mean(floats * floats, axis=-1, keepdims=True)
    return (floats * lax.rsqrt(mean_square + 1e-05) * gain).astype(BF16)


def kernel(
    x_ref, seg_ref, again_ref, qkv_ref, out_ref, fgain_ref, gate_ref, up_ref, down_ref,
    y_ref,
    xg, rg, pa, pb, across_a, across_b, far_a, far_b, near_a, near_b,
    wq, wo, wg, wu, wd, queries, kpad, vpad, mixed, bias, normed, segs, final, share, rounded, handed,
    send_sem, recv_sem, local_sem,
):
    half, width = xg.shape[1], xg.shape[2]
    chunk = 4 * half
    x, zh = lax.axis_index("x"), lax.axis_index("zh")
    core, y, zl = lax.axis_index("core"), lax.axis_index("y"), lax.axis_index("zl")
    nx, nzh = lax.axis_size("x"), lax.axis_size("zh")
    other = 1 - core
    pair_z = 1 - zl
    far_zh = lax.rem(zh + 2 * zl - 1 + nzh, nzh)
    wrong = lax.rem(core + zl, 2)

    def dev(zh_=zh, core_=core, y_=y, zl_=zl, x_=x):
        return (x_, zh_, core_, y_, zl_)

    def owner(y_):
        return dev(core_=core + wrong * (1 - 2 * core), y_=y_, zl_=zl + wrong * (1 - 2 * zl))

    up_y, down_y = lax.rem(y + 1, NY), lax.rem(y + NY - 1, NY)
    up_dev, down_dev = dev(y_=up_y), dev(y_=down_y)
    mate = dev(core_=other)
    beyond = dev(zh_=far_zh, zl_=pair_z)
    partner = dev(core_=other, zl_=pair_z)
    beside = (dev(x_=lax.rem(x + 1, nx)), dev(x_=lax.rem(x + nx - 1, nx)))

    def mine(dy):
        return 4 * lax.rem(y + dy, NY) + 2 * core

    def theirs(dy):
        return 4 * lax.rem(y + dy, NY) + 2 * other

    def copy(src, dst, slot, device):
        return pltpu.make_async_remote_copy(
            src_ref=src, dst_ref=dst, send_sem=send_sem.at[slot], recv_sem=recv_sem.at[slot],
            device_id=device, device_id_type=MESH,
        )

    def arrived(dst, slot):
        copy(dst, dst, slot, mate).wait_recv()

    def sent(src, slot):
        copy(src, src, slot, mate).wait_send()

    barrier = pltpu.get_barrier_semaphore()
    for device in (up_dev, down_dev, mate, beyond):
        pl.semaphore_signal(barrier, inc=1, device_id=device, device_id_type=MESH)

    @pl.when(wrong == 1)
    def _():
        for device in (partner, owner(up_y), owner(down_y)) + beside:
            pl.semaphore_signal(barrier, inc=1, device_id=device, device_id_type=MESH)

    pl.semaphore_wait(barrier, 4 + 5 * wrong)

    weights = ((qkv_ref, wq), (out_ref, wo), (gate_ref, wg), (up_ref, wu), (down_ref, wd))
    parity = lax.rem(x, 2)

    def rows_of(ref, at, piece, side):
        share_rows = ref.shape[0] // 2
        size = share_rows // PIECES[at][0]
        return ref.at[pl.ds(pl.multiple_of(side * share_rows + piece * size, 16), size)]

    def weight_wait(at):
        src, dst = weights[at]

        @pl.when(wrong == 0)
        def _():
            pltpu.make_async_copy(src, dst, local_sem.at[at]).wait()

        @pl.when(wrong == 1)
        def _():
            for piece in range(PIECES[at][0]):
                arrived(rows_of(dst, at, piece, 1 - parity), OVER_X + BEFORE[at] + piece)

    def send_weights(from_beyond, device):
        for at, (src, dst) in enumerate(weights):
            for piece in range(PIECES[at][0]):
                if (piece < PIECES[at][1]) == from_beyond:
                    copy(
                        rows_of(src, at, piece, parity), rows_of(dst, at, piece, parity),
                        NEAR_Z + BEFORE[at] + piece, device,
                    ).start()

    def weights_sent(from_beyond):
        for at, (src, dst) in enumerate(weights):
            for piece in range(PIECES[at][0]):
                if (piece < PIECES[at][1]) == from_beyond:
                    sent(rows_of(dst, at, piece, parity), NEAR_Z + BEFORE[at] + piece)

    def hand_on(at, *pieces):
        @pl.when(wrong == 1)
        def _():
            for piece in pieces:
                part = rows_of(weights[at][1], at, piece, parity)
                arrived(part, NEAR_Z + BEFORE[at] + piece)
                copy(part, part, OVER_X + BEFORE[at] + piece, beside[piece % 2]).start()

    cut = width // 256 * 128
    runs = (pl.ds(0, cut), pl.ds(cut, width - cut))

    def run_of(buf, at, side):
        return buf.at[at, :, runs[side]]

    own = mine(0)

    @pl.when(wrong == 0)
    def _():
        for piece in range(2):
            pltpu.make_async_copy(
                x_ref.at[pl.ds(piece * half, half)], xg.at[own + piece], local_sem.at[5 + piece]
            ).start()
        copy(seg_ref, segs, SEGS, mate).start()
        send_weights(True, beyond)
        for at, (src, dst) in enumerate(weights):
            pltpu.make_async_copy(src, dst, local_sem.at[at]).start()
        segs[...] = seg_ref[...]

    @pl.when(wrong == 1)
    def _():
        for p in range(2):
            for side in range(2):
                copy(
                    x_ref.at[pl.ds(p * half, half), runs[side]], run_of(xg, theirs(0) + p, side),
                    SWAP + 2 * p + side, partner,
                ).start()
        send_weights(False, partner)

    def spread(buf, base, at, side, slot, device):
        piece = run_of(buf, at, side)
        copy(piece, piece, base + slot, device).start()

    def cross(buf, base, p, dy, side):
        spread(buf, base, mine(dy) + p, side, ACROSS + 2 * dy + side, mate)

    def crossed(buf, base, dy, p):
        base = base + p * GATHER
        for side in range(2):
            arrived(run_of(buf, theirs(dy) + p, side), base + ACROSS + 2 * dy + side)

    def gather_start(buf, base, p, ready=lambda side: None):
        base = base + p * GATHER
        ready(0)
        spread(buf, base, own + p, 0, UP, up_dev)
        cross(buf, base, p, 0, 0)
        ready(1)
        spread(buf, base, own + p, 1, DOWN, down_dev)
        cross(buf, base, p, 0, 1)
        spread(buf, base, own + p, 1, UP + 1, up_dev)
        spread(buf, base, own + p, 0, DOWN + 1, down_dev)

    def gather_forward(buf, base, p):
        base = base + p * GATHER
        arrived(run_of(buf, mine(3) + p, 0), base + UP)
        spread(buf, base, mine(3) + p, 0, UP + 2, up_dev)
        cross(buf, base, p, 3, 0)
        arrived(run_of(buf, mine(1) + p, 1), base + DOWN)
        spread(buf, base, mine(1) + p, 1, DOWN + 2, down_dev)
        cross(buf, base, p, 1, 1)

    def gather_near(buf, base, p):
        base = base + p * GATHER
        arrived(run_of(buf, mine(3) + p, 1), base + UP + 1)
        cross(buf, base, p, 3, 1)
        arrived(run_of(buf, mine(1) + p, 0), base + DOWN + 1)
        cross(buf, base, p, 1, 0)

    def gather_far(buf, base, p):
        base = base + p * GATHER
        arrived(run_of(buf, mine(2) + p, 0), base + UP + 2)
        cross(buf, base, p, 2, 0)
        arrived(run_of(buf, mine(2) + p, 1), base + DOWN + 2)
        cross(buf, base, p, 2, 1)

    def gather_sent(buf, base):
        for p in range(2):
            for dy in range(4):
                for side in range(2):
                    sent(run_of(buf, own, side), base + p * GATHER + ACROSS + 2 * dy + side)
            for slot, side in ((UP, 0), (UP + 1, 1), (UP + 2, 0), (DOWN, 1), (DOWN + 1, 0), (DOWN + 2, 1)):
                sent(run_of(buf, own, side), base + p * GATHER + slot)

    def exchange(part, acc, base, p, dy):
        copy(part.at[theirs(dy) + p], acc.at[dy, p], base + p * REDUCE + dy, mate).start()

    def met(part, acc, p, dy, cols):
        return part[mine(dy) + p, :, cols].astype(F32) + acc[dy, p, :, cols].astype(F32)

    def reduce_far(part, acc, far, base, p):
        base = base + p * REDUCE
        arrived(acc.at[2, p], base + 2)
        for side, cols in enumerate(runs):
            at = mine(2) + p
            part[at, :, cols] = met(part, acc, p, 2, cols).astype(BF16)
            copy(
                run_of(part, at, side), run_of(far, p, side), base + FAR + side, (up_dev, down_dev)[side]
            ).start()

    def reduce_near(part, acc, far, near, base, p, dy, late, to=(up_dev, down_dev)):
        base = base + p * REDUCE
        way = 0 if dy == 1 else 1
        side = way if late else 1 - way
        at, cols = mine(dy) + p, runs[side]
        if late:
            arrived(run_of(far, p, side), base + FAR + side)
            part[at, :, cols] = (met(part, acc, p, dy, cols) + far[p, :, cols].astype(F32)).astype(BF16)
        else:
            arrived(acc.at[dy, p], base + dy)
            part[at, :, cols] = met(part, acc, p, dy, cols).astype(BF16)
        copy(
            run_of(part, at, side), near.at[way, p, :, cols], base + (NEAR_UP, NEAR_DOWN)[way] + side,
            to[way],
        ).start()

    def reduce_own(near, base, p, local, result):
        base = base + p * REDUCE
        for side, cols in enumerate(runs):
            for way in range(2):
                arrived(near.at[way, p, :, cols], base + (NEAR_UP, NEAR_DOWN)[way] + side)
            total = near[0, p, :, cols].astype(F32) + near[1, p, :, cols].astype(F32)
            result(cols, (local(cols) + total).astype(BF16))

    def reduce_sent(part, acc, base):
        for p in range(2):
            for dy in range(4):
                sent(acc.at[dy, p], base + p * REDUCE + dy)
            for slot in (FAR, NEAR_UP, NEAR_DOWN):
                for side in range(2):
                    sent(run_of(part, own, side), base + p * REDUCE + slot + side)

    def own_ready(p, side):
        if side == 0:
            @pl.when(wrong == 0)
            def _():
                pltpu.make_async_copy(
                    x_ref.at[pl.ds(p * half, half)], xg.at[own + p], local_sem.at[5 + p]
                ).wait()

        @pl.when(wrong == 1)
        def _():
            arrived(run_of(xg, own + p, side), SWAP + 2 * p + side)

    gather_start(xg, AG1, 0, functools.partial(own_ready, 0))
    hand_on(0, 0)
    gather_start(xg, AG1, 1, functools.partial(own_ready, 1))
    hand_on(0, 1)
    gather_forward(xg, AG1, 0)
    hand_on(0, 2, 4, 3)
    gather_forward(xg, AG1, 1)
    hand_on(0, 5)
    gather_near(xg, AG1, 0)
    hand_on(1, 0, 3, 1, 4)
    gather_near(xg, AG1, 1)
    hand_on(1, 2, 5)

    @pl.when(wrong == 1)
    def _():
        arrived(segs, SEGS)

    weight_wait(0)
    zeros = jnp.zeros((chunk, HEAD_DIM), BF16)

    def arrival(i):
        return lax.rem(3 * i + (i // 2) * (3 + 2 * lax.rem(i, 2)), NY)

    def project(i, carry):
        dy = arrival(i)
        u = lax.rem(y + dy, NY)

        @pl.when(i == 3)
        def _():
            gather_far(xg, AG1, 0)
            gather_far(xg, AG1, 1)

        crossed(xg, AG1, dy, 0)
        crossed(xg, AG1, dy, 1)
        rows = pl.ds(pl.multiple_of(u * chunk, chunk), chunk)
        normed[...] = norm_rows(xg[pl.ds(4 * u, 4)].reshape(chunk, width), again_ref[...])
        result = jnp.dot(normed[...], wq[...], preferred_element_type=F32).astype(BF16)
        for piece in range(4):
            queries[piece % 2, u, piece // 2] = result[piece * half : (piece + 1) * half, :Q_COLS]
        keys = result[:, Q_COLS : Q_COLS + HEAD_DIM]
        values = result[:, Q_COLS + HEAD_DIM :]
        kpad[0, rows, :] = jnp.concatenate([keys, zeros], axis=1)
        kpad[1, rows, :] = jnp.concatenate([zeros, keys], axis=1)
        vpad[0, rows, :] = jnp.concatenate([values, zeros], axis=1)
        vpad[1, rows, :] = jnp.concatenate([zeros, values], axis=1)
        return carry

    lax.fori_loop(0, NY, project, 0)

    rows_now = 2 * half

    def attend(at, p):
        seen = (at + 1) * chunk
        query_seg = jnp.broadcast_to(segs[:, at * chunk : seen], (128, chunk)).T[:, :1]
        query_seg = jnp.concatenate(
            [query_seg[(2 * c + p) * half : (2 * c + p + 1) * half] for c in range(2)], axis=0
        )
        row = lax.broadcasted_iota(jnp.int32, (rows_now, seen), 0)
        query_pos = at * chunk + p * half + row + jnp.where(row >= half, half, 0)
        key_pos = lax.broadcasted_iota(jnp.int32, (rows_now, seen), 1)
        allowed = (key_pos <= query_pos) & (segs[:, :seen] == query_seg)
        bias[:, :seen] = jnp.where(allowed, 0.0, -1e30)
        lane = lax.broadcasted_iota(jnp.int32, (rows_now, 128), 1)

        def heads(j, carry):
            cols = pl.ds(pl.multiple_of(j * 128, 128), 128)
            query = queries[p, at, :, :, cols].reshape(rows_now, 128)
            total, norm = None, []
            for side in range(2):
                scores = dot_t(query, kpad[side, :seen, :])
                scores = scores * HEAD_DIM ** (-0.5) + bias[:, :seen]
                weight = jnp.exp(scores - jnp.max(scores, axis=-1, keepdims=True))
                norm.append(jnp.sum(weight, axis=-1, keepdims=True))
                value = jnp.dot(weight.astype(BF16), vpad[side, :seen, :], preferred_element_type=F32)
                total = value if total is None else total + value
            mixed[:, cols] = (total / jnp.where(lane < HEAD_DIM, norm[0], norm[1])).astype(BF16)
            return carry

        lax.fori_loop(0, Q_COLS // 128, heads, 0, unroll=4)

    def put(part, u, p, left, right):
        for lo, size in tiles(width, 640):
            block = dot_t(left, right[lo : lo + size, :]).astype(BF16)
            for c in range(2):
                part[4 * u + 2 * c + p, :, lo : lo + size] = block[c * half : (c + 1) * half]

    def attention_step(p, i, carry):
        dy = lax.rem(2 + i + (i // 2) * (1 - 2 * lax.rem(i, 2)), NY)
        u = lax.rem(y + dy, NY)
        for at in range(NY):
            @pl.when(u == at)
            def _():
                attend(at, p)

        if p == 0:
            @pl.when(i == 0)
            def _():
                weight_wait(1)

            for at in (2, 3, 4):
                @pl.when(i == at - 1)
                def _():
                    hand_on(at, 0, 1)

        @pl.when(i == 1)
        def _():
            reduce_far(pa, across_a, far_a, RS1, p)
            if p == 1:
                reduce_near(pa, across_a, far_a, near_a, RS1, 0, 3, True)
                reduce_near(pa, across_a, far_a, near_a, RS1, 0, 1, True)

        @pl.when(i == 2)
        def _():
            reduce_near(pa, across_a, far_a, near_a, RS1, p, 3, False)

        @pl.when(i == 3)
        def _():
            reduce_near(pa, across_a, far_a, near_a, RS1, p, 1, False)

        put(pa, u, p, mixed[...], wo)
        exchange(pa, across_a, RS1, p, dy)
        return carry

    lax.fori_loop(0, NY, functools.partial(attention_step, 0), 0)
    lax.fori_loop(0, NY, functools.partial(attention_step, 1), 0)

    def resid_ready(p):
        def result(cols, value):
            rg[own + p, :, cols] = value

        def local(cols):
            return xg[own + p, :, cols].astype(F32) + met(pa, across_a, p, 0, cols)

        arrived(across_a.at[0, p], RS1 + p * REDUCE)
        reduce_own(near_a, RS1, p, local, result)

    resid_ready(0)
    gather_start(rg, AG2, 0)
    reduce_near(pa, across_a, far_a, near_a, RS1, 1, 3, True)
    reduce_near(pa, across_a, far_a, near_a, RS1, 1, 1, True)
    gather_forward(rg, AG2, 0)
    resid_ready(1)
    gather_start(rg, AG2, 1)
    for at in (2, 3, 4):
        weight_wait(at)

    owners = (owner(up_y), owner(down_y))

    def hand_over(p):
        arrived(across_b.at[0, p], RS2 + p * REDUCE)
        for cols in runs:
            total = rg[own + p, :, cols].astype(F32) + met(pb, across_b, p, 0, cols)
            share[p, :, cols] = total

        @pl.when(wrong == 1)
        def _():
            rounded[p] = share[p].astype(BF16)
            copy(rounded.at[p], handed.at[p], BACK + p, partner).start()

    def ffn_step(p, i, carry):
        dy = arrival(i)
        u = lax.rem(y + dy, NY)

        @pl.when(i == 1)
        def _():
            gather_near(rg, AG2, p)
            if p == 0:
                gather_forward(rg, AG2, 1)

        @pl.when(i == 3)
        def _():
            gather_far(rg, AG2, p)

        crossed(rg, AG2, dy, p)
        rows_in = jnp.concatenate([rg[4 * u + p], rg[4 * u + 2 + p]], axis=0)
        normed[:rows_now, :] = norm_rows(rows_in, fgain_ref[...])
        rows_in = normed[:rows_now, :]
        gate = jnp.dot(rows_in, wg[...], preferred_element_type=F32)
        lift = jnp.dot(rows_in, wu[...], preferred_element_type=F32)
        hidden = (gate / (1.0 + jnp.exp(-gate)) * lift).astype(BF16)
        put(pb, u, p, hidden, wd)
        exchange(pb, across_b, RS2, p, dy)
        if p == 1:
            @pl.when(i == 0)
            def _():
                reduce_far(pb, across_b, far_b, RS2, 0)

        @pl.when(i == 2)
        def _():
            reduce_near(pb, across_b, far_b, near_b, RS2, p, 3, False, owners)
            hand_over(p)
            if p == 1:
                reduce_near(pb, across_b, far_b, near_b, RS2, 0, 3, True, owners)
                reduce_near(pb, across_b, far_b, near_b, RS2, 0, 1, True, owners)

        @pl.when(i == 3)
        def _():
            reduce_near(pb, across_b, far_b, near_b, RS2, p, 1, False, owners)

        return carry

    lax.fori_loop(0, NY, functools.partial(ffn_step, 0), 0)
    lax.fori_loop(0, NY, functools.partial(ffn_step, 1), 0)

    def finish(p):
        def result(cols, value):
            final[p, :, cols] = value

        @pl.when(wrong == 1)
        def _():
            arrived(handed.at[p], BACK + p)
            share[p] = handed[p].astype(F32)

        reduce_own(near_b, RS2, p, lambda cols: share[p, :, cols], result)
        pltpu.make_async_copy(final.at[p], y_ref.at[pl.ds(p * half, half)], local_sem.at[7 + p]).start()

    reduce_far(pb, across_b, far_b, RS2, 1)
    finish(0)
    reduce_near(pb, across_b, far_b, near_b, RS2, 1, 3, True, owners)
    reduce_near(pb, across_b, far_b, near_b, RS2, 1, 1, True, owners)
    finish(1)

    gather_sent(xg, AG1)
    gather_sent(rg, AG2)
    reduce_sent(pa, across_a, RS1)
    reduce_sent(pb, across_b, RS2)

    @pl.when(wrong == 0)
    def _():
        sent(segs, SEGS)
        weights_sent(True)

    @pl.when(wrong == 1)
    def _():
        weights_sent(False)
        for at, (src, dst) in enumerate(weights):
            for piece in range(PIECES[at][0]):
                sent(rows_of(dst, at, piece, parity), OVER_X + BEFORE[at] + piece)
        for p in range(2):
            for side in range(2):
                sent(run_of(xg, own + p, side), SWAP + 2 * p + side)
            sent(rounded.at[p], BACK + p)

    for p in range(2):
        pltpu.make_async_copy(final.at[p], y_ref.at[pl.ds(p * half, half)], local_sem.at[7 + p]).wait()


def shards(
    activations, segment_ids, attn_gain, qkv_weight, out_weight, ffn_gain, gate_weight, up_weight, down_weight
):
    rows, width = activations.shape
    half, tokens = rows // 2, rows * 8
    chunk = 2 * rows
    vmem = pltpu.VMEM
    whole = pl.BlockSpec(memory_space=pltpu.VMEM)
    away = pl.BlockSpec(memory_space=pl.ANY)
    return pl.pallas_call(
        kernel,
        out_shape=jax.ShapeDtypeStruct((rows, width), BF16),
        in_specs=[away, whole, whole, away, away, whole, away, away, away],
        out_specs=away,
        scratch_shapes=[
            vmem((16, half, width), BF16),
            vmem((16, half, width), BF16),
            vmem((16, half, width), BF16),
            vmem((16, half, width), BF16),
            vmem((4, 2, half, width), BF16),
            vmem((4, 2, half, width), BF16),
            vmem((2, half, width), BF16),
            vmem((2, half, width), BF16),
            vmem((2, 2, half, width), BF16),
            vmem((2, 2, half, width), BF16),
            vmem(qkv_weight.shape, BF16),
            vmem(out_weight.shape[::-1], BF16),
            vmem(gate_weight.shape, BF16),
            vmem(up_weight.shape, BF16),
            vmem(down_weight.shape[::-1], BF16),
            vmem((2, NY, 2, half, Q_COLS), BF16),
            vmem((2, tokens, 128), BF16),
            vmem((2, tokens, 128), BF16),
            vmem((rows, Q_COLS), BF16),
            vmem((rows, tokens), F32),
            vmem((chunk, width), BF16),
            vmem((1, tokens), jnp.int32),
            vmem((2, half, width), BF16),
            vmem((2, half, width), F32),
            vmem((2, half, width), BF16),
            vmem((2, half, width), BF16),
            pltpu.SemaphoreType.DMA((SLOTS,)),
            pltpu.SemaphoreType.DMA((SLOTS,)),
            pltpu.SemaphoreType.DMA((9,)),
        ],
        compiler_params=pltpu.CompilerParams(
            collective_id=0, has_side_effects=True, vmem_limit_bytes=67043328
        ),
    )(
        activations, segment_ids.reshape(1, tokens), attn_gain, qkv_weight, out_weight.T,
        ffn_gain, gate_weight, up_weight, down_weight.T,
    )


def solution(mesh):
    groups = mesh.shape["dp"] // 8
    torus = Mesh(mesh.devices.reshape(4, groups, 2, NY, 2), AXES)
    dp, tensor = ("x", "zh", "core"), ("y", "zl")
    in_specs = (
        P(dp + tensor, None), P(dp), P(), P(None, tensor), P(tensor, None), P(),
        P(None, tensor), P(None, tensor), P(tensor, None),
    )
    return jax.shard_map(
        shards, mesh=torus, in_specs=in_specs, out_specs=P(dp + tensor, None), check_vma=False
    )
```

```python
import functools

import jax
import jax.numpy as jnp
from jax import lax
from jax.experimental import pallas as pl
from jax.experimental.pallas import tpu as pltpu
from jax.sharding import Mesh
from jax.sharding import PartitionSpec as P

HEAD_DIM = 64
Q_COLS = 512
AXES = ("x", "zh", "core", "y", "zl")
NY = 4
MESH = pl.DeviceIdType.MESH
F32 = jnp.float32
BF16 = jnp.bfloat16

UP, DOWN, ACROSS, GATHER = 0, 3, 6, 14
FAR, NEAR_UP, NEAR_DOWN, REDUCE = 8, 10, 12, 14
AG1 = 0
RS1 = AG1 + 2 * GATHER
AG2 = RS1 + 2 * REDUCE
RS2 = AG2 + 2 * GATHER
SWAP = RS2 + 2 * REDUCE
BACK = SWAP + 4
SEGS = BACK + 2
NEAR_Z = SEGS + 1
PIECES = ((6, 4), (6, 3), (2, 1), (2, 1), (2, 1))
BEFORE = (0, 6, 12, 14, 16)
OVER_X = NEAR_Z + 18
SLOTS = OVER_X + 18


def tiles(total, step):
    return [(at, min(step, total - at)) for at in range(0, total, step)]


def dot_t(left, right):
    return lax.dot_general(left, right, (((1,), (1,)), ((), ())), preferred_element_type=F32)


def norm_rows(rows, gain):
    floats = rows.astype(F32)
    mean_square = jnp.mean(floats * floats, axis=-1, keepdims=True)
    return (floats * lax.rsqrt(mean_square + 1e-05) * gain).astype(BF16)


def kernel(
    x_ref, seg_ref, again_ref, qkv_ref, out_ref, fgain_ref, gate_ref, up_ref, down_ref,
    y_ref,
    xg, rg, pa, pb, across_a, across_b, far_a, far_b, near_a, near_b,
    wq, wo, wg, wu, wd, queries, kpad, vpad, mixed, bias, normed, segs, final, share, rounded, handed, turned, staged,
    send_sem, recv_sem, local_sem,
):
    half, width = xg.shape[1], xg.shape[2]
    chunk = 4 * half
    x, zh = lax.axis_index("x"), lax.axis_index("zh")
    core, y, zl = lax.axis_index("core"), lax.axis_index("y"), lax.axis_index("zl")
    nx, nzh = lax.axis_size("x"), lax.axis_size("zh")
    other = 1 - core
    pair_z = 1 - zl
    far_zh = lax.rem(zh + 2 * zl - 1 + nzh, nzh)
    wrong = lax.rem(core + zl, 2)

    def dev(zh_=zh, core_=core, y_=y, zl_=zl, x_=x):
        return (x_, zh_, core_, y_, zl_)

    def owner(y_):
        return dev(core_=core + wrong * (1 - 2 * core), y_=y_, zl_=zl + wrong * (1 - 2 * zl))

    up_y, down_y = lax.rem(y + 1, NY), lax.rem(y + NY - 1, NY)
    up_dev, down_dev = dev(y_=up_y), dev(y_=down_y)
    mate = dev(core_=other)
    beyond = dev(zh_=far_zh, zl_=pair_z)
    partner = dev(core_=other, zl_=pair_z)
    beside = (dev(x_=lax.rem(x + 1, nx)), dev(x_=lax.rem(x + nx - 1, nx)))

    def mine(dy):
        return 4 * lax.rem(y + dy, NY) + 2 * core

    def theirs(dy):
        return 4 * lax.rem(y + dy, NY) + 2 * other

    def copy(src, dst, slot, device):
        return pltpu.make_async_remote_copy(
            src_ref=src, dst_ref=dst, send_sem=send_sem.at[slot], recv_sem=recv_sem.at[slot],
            device_id=device, device_id_type=MESH,
        )

    def arrived(dst, slot):
        copy(dst, dst, slot, mate).wait_recv()

    def sent(src, slot):
        copy(src, src, slot, mate).wait_send()

    whole_x = pltpu.make_async_copy(x_ref, turned, local_sem.at[5])
    whole_x.start()

    barrier = pltpu.get_barrier_semaphore()
    for device in (up_dev, down_dev, mate, beyond):
        pl.semaphore_signal(barrier, inc=1, device_id=device, device_id_type=MESH)

    @pl.when(wrong == 1)
    def _():
        for device in (partner, owner(up_y), owner(down_y)) + beside:
            pl.semaphore_signal(barrier, inc=1, device_id=device, device_id_type=MESH)


    weights = ((qkv_ref, wq), (out_ref, wo), (gate_ref, wg), (up_ref, wu), (down_ref, wd))
    parity = lax.rem(x, 2)

    def rows_of(ref, at, piece, side):
        share_rows = ref.shape[0] // 2
        size = share_rows // PIECES[at][0]
        return ref.at[pl.ds(pl.multiple_of(side * share_rows + piece * size, 16), size)]

    def weight_wait(at):
        src, dst = weights[at]

        @pl.when(wrong == 0)
        def _():
            pltpu.make_async_copy(src, dst, local_sem.at[at]).wait()

        @pl.when(wrong == 1)
        def _():
            for piece in range(PIECES[at][0]):
                arrived(rows_of(dst, at, piece, 1 - parity), OVER_X + BEFORE[at] + piece)

    def send_weights(from_beyond, device):
        for at, (src, dst) in enumerate(weights):
            for piece in range(PIECES[at][0]):
                if (piece < PIECES[at][1]) == from_beyond:
                    copy(
                        rows_of(src, at, piece, parity), rows_of(dst, at, piece, parity),
                        NEAR_Z + BEFORE[at] + piece, device,
                    ).start()

    def weights_sent(from_beyond):
        for at, (src, dst) in enumerate(weights):
            for piece in range(PIECES[at][0]):
                if (piece < PIECES[at][1]) == from_beyond:
                    sent(rows_of(dst, at, piece, parity), NEAR_Z + BEFORE[at] + piece)

    def hand_on(at, *pieces):
        @pl.when(wrong == 1)
        def _():
            for piece in pieces:
                part = rows_of(weights[at][1], at, piece, parity)
                arrived(part, NEAR_Z + BEFORE[at] + piece)
                copy(part, part, OVER_X + BEFORE[at] + piece, beside[piece % 2]).start()

    cut = width // 256 * 128
    runs = (pl.ds(0, cut), pl.ds(cut, width - cut))

    def run_of(buf, at, side):
        return buf.at[at, :, runs[side]]

    own = mine(0)

    whole_x.wait()

    def turn(into, base):
        for lo, size in tiles(width, 128):
            rows = turned[lo : lo + size, :].T
            for p in range(2):
                into[base + p, :, lo : lo + size] = rows[p * half : (p + 1) * half]

    @pl.when(wrong == 0)
    def _():
        turn(xg, own)

    @pl.when(wrong == 1)
    def _():
        turn(staged, 0)

    pl.semaphore_wait(barrier, 4 + 5 * wrong)

    @pl.when(wrong == 0)
    def _():
        copy(seg_ref, segs, SEGS, mate).start()
        send_weights(True, beyond)
        for at, (src, dst) in enumerate(weights):
            pltpu.make_async_copy(src, dst, local_sem.at[at]).start()
        segs[...] = seg_ref[...]

    @pl.when(wrong == 1)
    def _():
        for p in range(2):
            for side in range(2):
                copy(
                    run_of(staged, p, side), run_of(xg, theirs(0) + p, side), SWAP + 2 * p + side, partner
                ).start()
        send_weights(False, partner)

    def spread(buf, base, at, side, slot, device):
        piece = run_of(buf, at, side)
        copy(piece, piece, base + slot, device).start()

    def cross(buf, base, p, dy, side):
        spread(buf, base, mine(dy) + p, side, ACROSS + 2 * dy + side, mate)

    def crossed(buf, base, dy, p):
        base = base + p * GATHER
        for side in range(2):
            arrived(run_of(buf, theirs(dy) + p, side), base + ACROSS + 2 * dy + side)

    def gather_start(buf, base, p, ready=lambda side: None):
        base = base + p * GATHER
        ready(0)
        spread(buf, base, own + p, 0, UP, up_dev)
        cross(buf, base, p, 0, 0)
        ready(1)
        spread(buf, base, own + p, 1, DOWN, down_dev)
        cross(buf, base, p, 0, 1)
        spread(buf, base, own + p, 1, UP + 1, up_dev)
        spread(buf, base, own + p, 0, DOWN + 1, down_dev)

    def gather_forward(buf, base, p):
        base = base + p * GATHER
        arrived(run_of(buf, mine(3) + p, 0), base + UP)
        spread(buf, base, mine(3) + p, 0, UP + 2, up_dev)
        cross(buf, base, p, 3, 0)
        arrived(run_of(buf, mine(1) + p, 1), base + DOWN)
        spread(buf, base, mine(1) + p, 1, DOWN + 2, down_dev)
        cross(buf, base, p, 1, 1)

    def gather_near(buf, base, p):
        base = base + p * GATHER
        arrived(run_of(buf, mine(3) + p, 1), base + UP + 1)
        cross(buf, base, p, 3, 1)
        arrived(run_of(buf, mine(1) + p, 0), base + DOWN + 1)
        cross(buf, base, p, 1, 0)

    def gather_far(buf, base, p):
        base = base + p * GATHER
        arrived(run_of(buf, mine(2) + p, 0), base + UP + 2)
        cross(buf, base, p, 2, 0)
        arrived(run_of(buf, mine(2) + p, 1), base + DOWN + 2)
        cross(buf, base, p, 2, 1)

    def gather_sent(buf, base):
        for p in range(2):
            for dy in range(4):
                for side in range(2):
                    sent(run_of(buf, own, side), base + p * GATHER + ACROSS + 2 * dy + side)
            for slot, side in ((UP, 0), (UP + 1, 1), (UP + 2, 0), (DOWN, 1), (DOWN + 1, 0), (DOWN + 2, 1)):
                sent(run_of(buf, own, side), base + p * GATHER + slot)

    def exchange(part, acc, base, p, dy, side):
        copy(
            run_of(part, theirs(dy) + p, side), acc.at[dy, p, :, runs[side]],
            base + p * REDUCE + 2 * dy + side, mate,
        ).start()

    def exchanged(acc, base, p, dy, side):
        arrived(acc.at[dy, p, :, runs[side]], base + p * REDUCE + 2 * dy + side)

    def met(part, acc, p, dy, cols):
        return part[mine(dy) + p, :, cols].astype(F32) + acc[dy, p, :, cols].astype(F32)

    def reduce_far(part, acc, far, base, p):
        for side, cols in enumerate(runs):
            exchanged(acc, base, p, 2, side)
            at = mine(2) + p
            part[at, :, cols] = met(part, acc, p, 2, cols).astype(BF16)
            copy(
                run_of(part, at, side), run_of(far, p, side), base + p * REDUCE + FAR + side,
                (up_dev, down_dev)[side],
            ).start()

    def reduce_near(part, acc, far, near, base, p, dy, late, to=(up_dev, down_dev)):
        way = 0 if dy == 1 else 1
        side = way if late else 1 - way
        at, cols = mine(dy) + p, runs[side]
        exchanged(acc, base, p, dy, side)
        base = base + p * REDUCE
        if late:
            arrived(run_of(far, p, side), base + FAR + side)
            part[at, :, cols] = (met(part, acc, p, dy, cols) + far[p, :, cols].astype(F32)).astype(BF16)
        else:
            part[at, :, cols] = met(part, acc, p, dy, cols).astype(BF16)
        copy(
            run_of(part, at, side), near.at[way, p, :, cols], base + (NEAR_UP, NEAR_DOWN)[way] + side,
            to[way],
        ).start()

    def reduce_own(near, base, p, local, result):
        base = base + p * REDUCE
        for side, cols in enumerate(runs):
            for way in range(2):
                arrived(near.at[way, p, :, cols], base + (NEAR_UP, NEAR_DOWN)[way] + side)
            total = near[0, p, :, cols].astype(F32) + near[1, p, :, cols].astype(F32)
            result(cols, (local(cols) + total).astype(BF16))

    def reduce_sent(part, acc, base):
        for p in range(2):
            for slot in (0, 2, 4, 6, FAR, NEAR_UP, NEAR_DOWN):
                for side in range(2):
                    sent(run_of(part, own, side), base + p * REDUCE + slot + side)

    def own_ready(p, side):
        @pl.when(wrong == 1)
        def _():
            arrived(run_of(xg, own + p, side), SWAP + 2 * p + side)

    gather_start(xg, AG1, 0, functools.partial(own_ready, 0))
    hand_on(0, 0)
    gather_start(xg, AG1, 1, functools.partial(own_ready, 1))
    hand_on(0, 1)
    gather_forward(xg, AG1, 0)
    hand_on(0, 2, 4, 3)
    gather_forward(xg, AG1, 1)
    hand_on(0, 5)
    gather_near(xg, AG1, 0)
    hand_on(1, 0, 3, 1, 4)
    gather_near(xg, AG1, 1)
    hand_on(1, 2, 5)

    @pl.when(wrong == 1)
    def _():
        arrived(segs, SEGS)

    weight_wait(0)
    zeros = jnp.zeros((chunk, HEAD_DIM), BF16)

    def arrival(i):
        return lax.rem(3 * i + (i // 2) * (3 + 2 * lax.rem(i, 2)), NY)

    def project(i, carry):
        dy = arrival(i)
        u = lax.rem(y + dy, NY)

        @pl.when(i == 3)
        def _():
            gather_far(xg, AG1, 0)
            gather_far(xg, AG1, 1)

        crossed(xg, AG1, dy, 0)
        crossed(xg, AG1, dy, 1)
        rows = pl.ds(pl.multiple_of(u * chunk, chunk), chunk)
        normed[...] = norm_rows(xg[pl.ds(4 * u, 4)].reshape(chunk, width), again_ref[...])
        scale = jnp.asarray(HEAD_DIM ** (-0.5), BF16)
        result = jnp.dot(normed[...], wq[...], preferred_element_type=F32).astype(BF16)
        for piece in range(4):
            queries[piece % 2, u, piece // 2] = result[piece * half : (piece + 1) * half, :Q_COLS] * scale
        keys = result[:, Q_COLS : Q_COLS + HEAD_DIM]
        values = result[:, Q_COLS + HEAD_DIM :]
        kpad[0, rows, :] = jnp.concatenate([keys, zeros], axis=1)
        kpad[1, rows, :] = jnp.concatenate([zeros, keys], axis=1)
        vpad[0, rows, :] = jnp.concatenate([values, zeros], axis=1)
        vpad[1, rows, :] = jnp.concatenate([zeros, values], axis=1)
        return carry

    lax.fori_loop(0, NY, project, 0)

    rows_now = 2 * half

    def attend(at, p):
        seen = (at + 1) * chunk
        query_seg = jnp.broadcast_to(segs[:, at * chunk : seen], (128, chunk)).T[:, :1]
        query_seg = jnp.concatenate(
            [query_seg[(2 * c + p) * half : (2 * c + p + 1) * half] for c in range(2)], axis=0
        )
        row = lax.broadcasted_iota(jnp.int32, (rows_now, seen), 0)
        query_pos = at * chunk + p * half + row + jnp.where(row >= half, half, 0)
        key_pos = lax.broadcasted_iota(jnp.int32, (rows_now, seen), 1)
        allowed = (key_pos <= query_pos) & (segs[:, :seen] == query_seg)
        bias[:, :seen] = jnp.where(allowed, 0.0, -1e30)
        lane = lax.broadcasted_iota(jnp.int32, (rows_now, 128), 1)

        def heads(j, carry):
            cols = pl.ds(pl.multiple_of(j * 128, 128), 128)
            query = queries[p, at, :, :, cols].reshape(rows_now, 128)
            total, norm = None, []
            for side in range(2):
                scores = dot_t(query, kpad[side, :seen, :])
                scores = scores + bias[:, :seen]
                weight = jnp.exp(scores - jnp.max(scores, axis=-1, keepdims=True))
                norm.append(jnp.sum(weight, axis=-1, keepdims=True))
                value = jnp.dot(weight.astype(BF16), vpad[side, :seen, :], preferred_element_type=F32)
                total = value if total is None else total + value
            mixed[:, cols] = (total / jnp.where(lane < HEAD_DIM, norm[0], norm[1])).astype(BF16)
            return carry

        lax.fori_loop(0, Q_COLS // 128, heads, 0, unroll=4)

    def put(part, acc, base, dy, u, p, left, right):
        for side, (first, length) in enumerate(((0, cut), (cut, width - cut))):
            for at, size in tiles(length, 768):
                lo = first + at
                block = dot_t(left, right[lo : lo + size, :]).astype(BF16)
                for c in range(2):
                    part[4 * u + 2 * c + p, :, lo : lo + size] = block[c * half : (c + 1) * half]
            exchange(part, acc, base, p, dy, side)

    def resid_ready(p):
        def result(cols, value):
            rg[own + p, :, cols] = value

        def local(cols):
            return xg[own + p, :, cols].astype(F32) + met(pa, across_a, p, 0, cols)

        for side in range(2):
            exchanged(across_a, RS1, p, 0, side)
        reduce_own(near_a, RS1, p, local, result)

    def attention_step(p, i, carry):
        dy = lax.rem(2 + i + (i // 2) * (1 - 2 * lax.rem(i, 2)), NY)
        u = lax.rem(y + dy, NY)
        for at in range(NY):
            @pl.when(u == at)
            def _():
                attend(at, p)

        if p == 0:
            @pl.when(i == 0)
            def _():
                weight_wait(1)

            for at in (2, 3, 4):
                @pl.when(i == at - 1)
                def _():
                    hand_on(at, 0, 1)

        @pl.when(i == 1)
        def _():
            reduce_far(pa, across_a, far_a, RS1, p)

        @pl.when(i == 2)
        def _():
            reduce_near(pa, across_a, far_a, near_a, RS1, p, 3, False)

        @pl.when(i == 3)
        def _():
            reduce_near(pa, across_a, far_a, near_a, RS1, p, 1, False)
            reduce_near(pa, across_a, far_a, near_a, RS1, p, 3, True)
            reduce_near(pa, across_a, far_a, near_a, RS1, p, 1, True)
            if p == 1:
                resid_ready(0)
                gather_start(rg, AG2, 0)

        put(pa, across_a, RS1, dy, u, p, mixed[...], wo)
        return carry

    lax.fori_loop(0, NY, functools.partial(attention_step, 0), 0)
    lax.fori_loop(0, NY, functools.partial(attention_step, 1), 0)

    gather_forward(rg, AG2, 0)
    resid_ready(1)
    gather_start(rg, AG2, 1)
    for at in (2, 3, 4):
        weight_wait(at)

    owners = (owner(up_y), owner(down_y))

    def hand_over(p):
        for side in range(2):
            exchanged(across_b, RS2, p, 0, side)
        for cols in runs:
            total = rg[own + p, :, cols].astype(F32) + met(pb, across_b, p, 0, cols)
            share[p, :, cols] = total

        @pl.when(wrong == 1)
        def _():
            rounded[p] = share[p].astype(BF16)
            copy(rounded.at[p], handed.at[p], BACK + p, partner).start()

    def ffn_step(p, i, carry):
        dy = arrival(i)
        u = lax.rem(y + dy, NY)

        @pl.when(i == 1)
        def _():
            gather_near(rg, AG2, p)
            if p == 0:
                gather_forward(rg, AG2, 1)

        @pl.when(i == 3)
        def _():
            gather_far(rg, AG2, p)

        crossed(rg, AG2, dy, p)
        rows_in = jnp.concatenate([rg[4 * u + p], rg[4 * u + 2 + p]], axis=0)
        normed[:rows_now, :] = norm_rows(rows_in, fgain_ref[...])
        rows_in = normed[:rows_now, :]
        gate = jnp.dot(rows_in, wg[...], preferred_element_type=F32)
        lift = jnp.dot(rows_in, wu[...], preferred_element_type=F32)
        hidden = (gate / (1.0 + jnp.exp(-gate)) * lift).astype(BF16)
        put(pb, across_b, RS2, dy, u, p, hidden, wd)
        if p == 1:
            @pl.when(i == 0)
            def _():
                reduce_far(pb, across_b, far_b, RS2, 0)

        @pl.when(i == 2)
        def _():
            reduce_near(pb, across_b, far_b, near_b, RS2, p, 3, False, owners)
            hand_over(p)
            if p == 1:
                reduce_near(pb, across_b, far_b, near_b, RS2, 0, 3, True, owners)
                reduce_near(pb, across_b, far_b, near_b, RS2, 0, 1, True, owners)

        @pl.when(i == 3)
        def _():
            reduce_near(pb, across_b, far_b, near_b, RS2, p, 1, False, owners)

        return carry

    lax.fori_loop(0, NY, functools.partial(ffn_step, 0), 0)
    lax.fori_loop(0, NY, functools.partial(ffn_step, 1), 0)

    def finish(p):
        def result(cols, value):
            final[p, :, cols] = value

        @pl.when(wrong == 1)
        def _():
            arrived(handed.at[p], BACK + p)
            share[p] = handed[p].astype(F32)

        reduce_own(near_b, RS2, p, lambda cols: share[p, :, cols], result)

    reduce_far(pb, across_b, far_b, RS2, 1)
    finish(0)
    reduce_near(pb, across_b, far_b, near_b, RS2, 1, 3, True, owners)
    reduce_near(pb, across_b, far_b, near_b, RS2, 1, 1, True, owners)
    finish(1)

    for lo, size in tiles(width, 128):
        rows = jnp.concatenate([final[0, :, lo : lo + size], final[1, :, lo : lo + size]], axis=0)
        y_ref[lo : lo + size, :] = rows.T

    gather_sent(xg, AG1)
    gather_sent(rg, AG2)
    reduce_sent(pa, across_a, RS1)
    reduce_sent(pb, across_b, RS2)

    @pl.when(wrong == 0)
    def _():
        sent(segs, SEGS)
        weights_sent(True)

    @pl.when(wrong == 1)
    def _():
        weights_sent(False)
        for at, (src, dst) in enumerate(weights):
            for piece in range(PIECES[at][0]):
                sent(rows_of(dst, at, piece, parity), OVER_X + BEFORE[at] + piece)
        for p in range(2):
            for side in range(2):
                sent(run_of(xg, own + p, side), SWAP + 2 * p + side)
            sent(rounded.at[p], BACK + p)


def shards(
    activations, segment_ids, attn_gain, qkv_weight, out_weight, ffn_gain, gate_weight, up_weight, down_weight
):
    rows, width = activations.shape
    half, tokens = rows // 2, rows * 8
    chunk = 2 * rows
    vmem = pltpu.VMEM
    whole = pl.BlockSpec(memory_space=pltpu.VMEM)
    away = pl.BlockSpec(memory_space=pl.ANY)
    return pl.pallas_call(
        kernel,
        out_shape=pltpu.VMEM((width, rows), BF16),
        in_specs=[away, whole, whole, away, away, whole, away, away, away],
        out_specs=whole,
        scratch_shapes=[
            vmem((16, half, width), BF16),
            vmem((16, half, width), BF16),
            vmem((16, half, width), BF16),
            vmem((16, half, width), BF16),
            vmem((4, 2, half, width), BF16),
            vmem((4, 2, half, width), BF16),
            vmem((2, half, width), BF16),
            vmem((2, half, width), BF16),
            vmem((2, 2, half, width), BF16),
            vmem((2, 2, half, width), BF16),
            vmem(qkv_weight.shape, BF16),
            vmem(out_weight.shape[::-1], BF16),
            vmem(gate_weight.shape, BF16),
            vmem(up_weight.shape, BF16),
            vmem(down_weight.shape[::-1], BF16),
            vmem((2, NY, 2, half, Q_COLS), BF16),
            vmem((2, tokens, 128), BF16),
            vmem((2, tokens, 128), BF16),
            vmem((rows, Q_COLS), BF16),
            vmem((rows, tokens), F32),
            vmem((chunk, width), BF16),
            vmem((1, tokens), jnp.int32),
            vmem((2, half, width), BF16),
            vmem((2, half, width), F32),
            vmem((2, half, width), BF16),
            vmem((2, half, width), BF16),
            vmem((width, rows), BF16),
            vmem((2, half, width), BF16),
            pltpu.SemaphoreType.DMA((SLOTS,)),
            pltpu.SemaphoreType.DMA((SLOTS,)),
            pltpu.SemaphoreType.DMA((7,)),
        ],
        compiler_params=pltpu.CompilerParams(
            collective_id=0, has_side_effects=True, vmem_limit_bytes=64000000
        ),
    )(
        activations.T, segment_ids.reshape(1, tokens), attn_gain, qkv_weight, out_weight.T,
        ffn_gain, gate_weight, up_weight, down_weight.T,
    ).T


def solution(mesh):
    groups = mesh.shape["dp"] // 8
    torus = Mesh(mesh.devices.reshape(4, groups, 2, NY, 2), AXES)
    dp, tensor = ("x", "zh", "core"), ("y", "zl")
    in_specs = (
        P(dp + tensor, None), P(dp), P(), P(None, tensor), P(tensor, None), P(),
        P(None, tensor), P(None, tensor), P(tensor, None),
    )
    return jax.shard_map(
        shards, mesh=torus, in_specs=in_specs, out_specs=P(dp + tensor, None), check_vma=False
    )
```

```python
import functools

import jax
import jax.numpy as jnp
from jax import lax
from jax.experimental import pallas as pl
from jax.experimental.pallas import tpu as pltpu
from jax.sharding import Mesh
from jax.sharding import PartitionSpec as P

HEAD_DIM = 64
Q_COLS = 512
AXES = ("x", "zh", "core", "y", "zl")
NY = 4
MESH = pl.DeviceIdType.MESH
F32 = jnp.float32
BF16 = jnp.bfloat16

UP, DOWN, ACROSS, GATHER = 0, 3, 6, 14
FAR, NEAR_UP, NEAR_DOWN, REDUCE = 8, 10, 12, 14
AG1 = 0
RS1 = AG1 + 2 * GATHER
AG2 = RS1 + 2 * REDUCE
RS2 = AG2 + 2 * GATHER
SWAP = RS2 + 2 * REDUCE
BACK = SWAP + 4
SEGS = BACK + 2
NEAR_Z = SEGS + 1
PIECES = ((6, 4), (6, 3), (2, 1), (2, 1), (2, 1))
BEFORE = (0, 6, 12, 14, 16)
OVER_X = NEAR_Z + 18
SLOTS = OVER_X + 18


def tiles(total, step):
    return [(at, min(step, total - at)) for at in range(0, total, step)]


def dot_t(left, right):
    return lax.dot_general(left, right, (((1,), (1,)), ((), ())), preferred_element_type=F32)


def norm_rows(rows, gain):
    floats = rows.astype(F32)
    mean_square = jnp.mean(floats * floats, axis=-1, keepdims=True)
    return (floats * lax.rsqrt(mean_square + 1e-05) * gain).astype(BF16)


def kernel(
    x_ref, seg_ref, again_ref, qkv_ref, out_ref, fgain_ref, gate_ref, up_ref, down_ref,
    y_ref,
    xg, rg, pa, pb, across_a, across_b, far_a, far_b, near_a, near_b,
    wq, wo, wg, wu, wd, queries, kpad, vpad, mixed, bias, normed, segs, final, share, rounded, handed, turned, staged,
    send_sem, recv_sem, local_sem,
):
    half, width = xg.shape[1], xg.shape[2]
    chunk = 4 * half
    x, zh = lax.axis_index("x"), lax.axis_index("zh")
    core, y, zl = lax.axis_index("core"), lax.axis_index("y"), lax.axis_index("zl")
    nx, nzh = lax.axis_size("x"), lax.axis_size("zh")
    other = 1 - core
    pair_z = 1 - zl
    far_zh = lax.rem(zh + 2 * zl - 1 + nzh, nzh)
    wrong = lax.rem(core + zl, 2)

    def dev(zh_=zh, core_=core, y_=y, zl_=zl, x_=x):
        return (x_, zh_, core_, y_, zl_)

    def owner(y_):
        return dev(core_=core + wrong * (1 - 2 * core), y_=y_, zl_=zl + wrong * (1 - 2 * zl))

    up_y, down_y = lax.rem(y + 1, NY), lax.rem(y + NY - 1, NY)
    up_dev, down_dev = dev(y_=up_y), dev(y_=down_y)
    mate = dev(core_=other)
    beyond = dev(zh_=far_zh, zl_=pair_z)
    partner = dev(core_=other, zl_=pair_z)
    beside = (dev(x_=lax.rem(x + 1, nx)), dev(x_=lax.rem(x + nx - 1, nx)))

    def mine(dy):
        return 4 * lax.rem(y + dy, NY) + 2 * core

    def theirs(dy):
        return 4 * lax.rem(y + dy, NY) + 2 * other

    def copy(src, dst, slot, device):
        return pltpu.make_async_remote_copy(
            src_ref=src, dst_ref=dst, send_sem=send_sem.at[slot], recv_sem=recv_sem.at[slot],
            device_id=device, device_id_type=MESH,
        )

    def arrived(dst, slot):
        copy(dst, dst, slot, mate).wait_recv()

    def sent(src, slot):
        copy(src, src, slot, mate).wait_send()

    whole_x = pltpu.make_async_copy(x_ref, turned, local_sem.at[5])
    whole_x.start()

    barrier = pltpu.get_barrier_semaphore()
    for device in (up_dev, down_dev, mate, beyond):
        pl.semaphore_signal(barrier, inc=1, device_id=device, device_id_type=MESH)

    @pl.when(wrong == 1)
    def _():
        for device in (partner, owner(up_y), owner(down_y)) + beside:
            pl.semaphore_signal(barrier, inc=1, device_id=device, device_id_type=MESH)


    weights = ((qkv_ref, wq), (out_ref, wo), (gate_ref, wg), (up_ref, wu), (down_ref, wd))
    parity = lax.rem(x, 2)

    def rows_of(ref, at, piece, side):
        share_rows = ref.shape[0] // 2
        size = share_rows // PIECES[at][0]
        return ref.at[pl.ds(pl.multiple_of(side * share_rows + piece * size, 16), size)]

    def weight_wait(at):
        src, dst = weights[at]

        @pl.when(wrong == 0)
        def _():
            pltpu.make_async_copy(src, dst, local_sem.at[at]).wait()

        @pl.when(wrong == 1)
        def _():
            for piece in range(PIECES[at][0]):
                arrived(rows_of(dst, at, piece, 1 - parity), OVER_X + BEFORE[at] + piece)

    def send_weights(from_beyond, device):
        for at, (src, dst) in enumerate(weights):
            for piece in range(PIECES[at][0]):
                if (piece < PIECES[at][1]) == from_beyond:
                    copy(
                        rows_of(src, at, piece, parity), rows_of(dst, at, piece, parity),
                        NEAR_Z + BEFORE[at] + piece, device,
                    ).start()

    def weights_sent(from_beyond):
        for at, (src, dst) in enumerate(weights):
            for piece in range(PIECES[at][0]):
                if (piece < PIECES[at][1]) == from_beyond:
                    sent(rows_of(dst, at, piece, parity), NEAR_Z + BEFORE[at] + piece)

    def hand_on(at, *pieces):
        @pl.when(wrong == 1)
        def _():
            for piece in pieces:
                part = rows_of(weights[at][1], at, piece, parity)
                arrived(part, NEAR_Z + BEFORE[at] + piece)
                copy(part, part, OVER_X + BEFORE[at] + piece, beside[piece % 2]).start()

    cut = width // 256 * 128
    runs = (pl.ds(0, cut), pl.ds(cut, width - cut))

    def run_of(buf, at, side):
        return buf.at[at, :, runs[side]]

    own = mine(0)

    whole_x.wait()

    def turn(into, base):
        for lo, size in tiles(width, 128):
            rows = turned[lo : lo + size, :].T
            for p in range(2):
                into[base + p, :, lo : lo + size] = rows[p * half : (p + 1) * half]

    @pl.when(wrong == 0)
    def _():
        turn(xg, own)

    @pl.when(wrong == 1)
    def _():
        turn(staged, 0)

    pl.semaphore_wait(barrier, 4 + 5 * wrong)

    @pl.when(wrong == 0)
    def _():
        copy(seg_ref, segs, SEGS, mate).start()
        send_weights(True, beyond)
        for at, (src, dst) in enumerate(weights):
            pltpu.make_async_copy(src, dst, local_sem.at[at]).start()
        segs[...] = seg_ref[...]

    @pl.when(wrong == 1)
    def _():
        for p in range(2):
            for side in range(2):
                copy(
                    run_of(staged, p, side), run_of(xg, theirs(0) + p, side), SWAP + 2 * p + side, partner
                ).start()
        send_weights(False, partner)

    def spread(buf, base, at, side, slot, device):
        piece = run_of(buf, at, side)
        copy(piece, piece, base + slot, device).start()

    def cross(buf, base, p, dy, side):
        spread(buf, base, mine(dy) + p, side, ACROSS + 2 * dy + side, mate)

    def crossed(buf, base, dy, p):
        base = base + p * GATHER
        for side in range(2):
            arrived(run_of(buf, theirs(dy) + p, side), base + ACROSS + 2 * dy + side)

    def gather_start(buf, base, p, ready=lambda side: None):
        base = base + p * GATHER
        ready(0)
        spread(buf, base, own + p, 0, UP, up_dev)
        cross(buf, base, p, 0, 0)
        ready(1)
        spread(buf, base, own + p, 1, DOWN, down_dev)
        cross(buf, base, p, 0, 1)
        spread(buf, base, own + p, 1, UP + 1, up_dev)
        spread(buf, base, own + p, 0, DOWN + 1, down_dev)

    def gather_forward(buf, base, p):
        base = base + p * GATHER
        arrived(run_of(buf, mine(3) + p, 0), base + UP)
        spread(buf, base, mine(3) + p, 0, UP + 2, up_dev)
        cross(buf, base, p, 3, 0)
        arrived(run_of(buf, mine(1) + p, 1), base + DOWN)
        spread(buf, base, mine(1) + p, 1, DOWN + 2, down_dev)
        cross(buf, base, p, 1, 1)

    def gather_near(buf, base, p):
        base = base + p * GATHER
        arrived(run_of(buf, mine(3) + p, 1), base + UP + 1)
        cross(buf, base, p, 3, 1)
        arrived(run_of(buf, mine(1) + p, 0), base + DOWN + 1)
        cross(buf, base, p, 1, 0)

    def gather_far(buf, base, p):
        base = base + p * GATHER
        arrived(run_of(buf, mine(2) + p, 0), base + UP + 2)
        cross(buf, base, p, 2, 0)
        arrived(run_of(buf, mine(2) + p, 1), base + DOWN + 2)
        cross(buf, base, p, 2, 1)

    def gather_sent(buf, base):
        for p in range(2):
            for dy in range(4):
                for side in range(2):
                    sent(run_of(buf, own, side), base + p * GATHER + ACROSS + 2 * dy + side)
            for slot, side in ((UP, 0), (UP + 1, 1), (UP + 2, 0), (DOWN, 1), (DOWN + 1, 0), (DOWN + 2, 1)):
                sent(run_of(buf, own, side), base + p * GATHER + slot)

    def exchange(part, acc, base, p, dy, side):
        copy(
            run_of(part, theirs(dy) + p, side), acc.at[dy, p, :, runs[side]],
            base + p * REDUCE + 2 * dy + side, mate,
        ).start()

    def exchanged(acc, base, p, dy, side):
        arrived(acc.at[dy, p, :, runs[side]], base + p * REDUCE + 2 * dy + side)

    def met(part, acc, p, dy, cols):
        return part[mine(dy) + p, :, cols].astype(F32) + acc[dy, p, :, cols].astype(F32)

    def reduce_far(part, acc, far, base, p):
        for side, cols in enumerate(runs):
            exchanged(acc, base, p, 2, side)
            at = mine(2) + p
            part[at, :, cols] = met(part, acc, p, 2, cols).astype(BF16)
            copy(
                run_of(part, at, side), run_of(far, p, side), base + p * REDUCE + FAR + side,
                (up_dev, down_dev)[side],
            ).start()

    def reduce_near(part, acc, far, near, base, p, dy, late, to=(up_dev, down_dev)):
        way = 0 if dy == 1 else 1
        side = way if late else 1 - way
        at, cols = mine(dy) + p, runs[side]
        exchanged(acc, base, p, dy, side)
        base = base + p * REDUCE
        if late:
            arrived(run_of(far, p, side), base + FAR + side)
            part[at, :, cols] = (met(part, acc, p, dy, cols) + far[p, :, cols].astype(F32)).astype(BF16)
        else:
            part[at, :, cols] = met(part, acc, p, dy, cols).astype(BF16)
        copy(
            run_of(part, at, side), near.at[way, p, :, cols], base + (NEAR_UP, NEAR_DOWN)[way] + side,
            to[way],
        ).start()

    def reduce_own(near, base, p, local, result):
        base = base + p * REDUCE
        for side, cols in enumerate(runs):
            for way in range(2):
                arrived(near.at[way, p, :, cols], base + (NEAR_UP, NEAR_DOWN)[way] + side)
            total = near[0, p, :, cols].astype(F32) + near[1, p, :, cols].astype(F32)
            result(cols, (local(cols) + total).astype(BF16))

    def reduce_sent(part, acc, base):
        for p in range(2):
            for slot in (0, 2, 4, 6, FAR, NEAR_UP, NEAR_DOWN):
                for side in range(2):
                    sent(run_of(part, own, side), base + p * REDUCE + slot + side)

    def own_ready(p, side):
        @pl.when(wrong == 1)
        def _():
            arrived(run_of(xg, own + p, side), SWAP + 2 * p + side)

    gather_start(xg, AG1, 0, functools.partial(own_ready, 0))
    hand_on(0, 0)
    gather_start(xg, AG1, 1, functools.partial(own_ready, 1))
    hand_on(0, 1)
    gather_forward(xg, AG1, 0)
    hand_on(0, 2, 4, 3)
    gather_forward(xg, AG1, 1)
    hand_on(0, 5)
    gather_near(xg, AG1, 0)
    hand_on(1, 0, 3, 1, 4)
    gather_near(xg, AG1, 1)
    hand_on(1, 2, 5)

    @pl.when(wrong == 1)
    def _():
        arrived(segs, SEGS)

    weight_wait(0)
    zeros = jnp.zeros((chunk, HEAD_DIM), BF16)

    def arrival(i):
        return lax.rem(3 * i + (i // 2) * (3 + 2 * lax.rem(i, 2)), NY)

    def project(i, carry):
        dy = arrival(i)
        u = lax.rem(y + dy, NY)

        @pl.when(i == 3)
        def _():
            gather_far(xg, AG1, 0)
            gather_far(xg, AG1, 1)

        crossed(xg, AG1, dy, 0)
        crossed(xg, AG1, dy, 1)
        rows = pl.ds(pl.multiple_of(u * chunk, chunk), chunk)
        normed[...] = norm_rows(xg[pl.ds(4 * u, 4)].reshape(chunk, width), again_ref[...])
        scale = jnp.asarray(HEAD_DIM ** (-0.5), BF16)
        result = jnp.dot(normed[...], wq[...], preferred_element_type=F32).astype(BF16)
        for piece in range(4):
            queries[piece % 2, u, piece // 2] = result[piece * half : (piece + 1) * half, :Q_COLS] * scale
        keys = result[:, Q_COLS : Q_COLS + HEAD_DIM]
        values = result[:, Q_COLS + HEAD_DIM :]
        kpad[0, rows, :] = jnp.concatenate([keys, zeros], axis=1)
        kpad[1, rows, :] = jnp.concatenate([zeros, keys], axis=1)
        vpad[0, rows, :] = jnp.concatenate([values, zeros], axis=1)
        vpad[1, rows, :] = jnp.concatenate([zeros, values], axis=1)
        return carry

    lax.fori_loop(0, NY, project, 0)

    rows_now = 2 * half

    def attend(at, p):
        seen = (at + 1) * chunk
        query_seg = jnp.broadcast_to(segs[:, at * chunk : seen], (128, chunk)).T[:, :1]
        query_seg = jnp.concatenate(
            [query_seg[(2 * c + p) * half : (2 * c + p + 1) * half] for c in range(2)], axis=0
        )
        row = lax.broadcasted_iota(jnp.int32, (rows_now, seen), 0)
        query_pos = at * chunk + p * half + row + jnp.where(row >= half, half, 0)
        key_pos = lax.broadcasted_iota(jnp.int32, (rows_now, seen), 1)
        allowed = (key_pos <= query_pos) & (segs[:, :seen] == query_seg)
        bias[:, :seen] = jnp.where(allowed, 0.0, -1e30)
        lane = lax.broadcasted_iota(jnp.int32, (rows_now, 128), 1)

        def heads(j, carry):
            cols = pl.ds(pl.multiple_of(j * 128, 128), 128)
            query = queries[p, at, :, :, cols].reshape(rows_now, 128)
            total, norm = None, []
            for side in range(2):
                scores = dot_t(query, kpad[side, :seen, :])
                scores = scores + bias[:, :seen]
                weight = jnp.exp(scores - jnp.max(scores, axis=-1, keepdims=True))
                norm.append(jnp.sum(weight, axis=-1, keepdims=True))
                value = jnp.dot(weight.astype(BF16), vpad[side, :seen, :], preferred_element_type=F32)
                total = value if total is None else total + value
            mixed[:, cols] = (total / jnp.where(lane < HEAD_DIM, norm[0], norm[1])).astype(BF16)
            return carry

        lax.fori_loop(0, Q_COLS // 128, heads, 0, unroll=4)

    def put(part, acc, base, dy, u, p, left, right):
        for side, (first, length) in enumerate(((0, cut), (cut, width - cut))):
            for at, size in tiles(length, 768):
                lo = first + at
                block = dot_t(left, right[lo : lo + size, :]).astype(BF16)
                for c in range(2):
                    part[4 * u + 2 * c + p, :, lo : lo + size] = block[c * half : (c + 1) * half]
            exchange(part, acc, base, p, dy, side)

    def resid_ready(p):
        def result(cols, value):
            rg[own + p, :, cols] = value

        def local(cols):
            return xg[own + p, :, cols].astype(F32) + met(pa, across_a, p, 0, cols)

        for side in range(2):
            exchanged(across_a, RS1, p, 0, side)
        reduce_own(near_a, RS1, p, local, result)

    def attention_step(p, i, carry):
        dy = lax.rem(2 + i + (i // 2) * (1 - 2 * lax.rem(i, 2)), NY)
        u = lax.rem(y + dy, NY)
        for at in range(NY):
            @pl.when(u == at)
            def _():
                attend(at, p)

        if p == 0:
            @pl.when(i == 0)
            def _():
                weight_wait(1)

            for at in (2, 3, 4):
                @pl.when(i == at - 1)
                def _():
                    hand_on(at, 0, 1)

        @pl.when(i == 1)
        def _():
            if p == 1:
                reduce_far(pa, across_a, far_a, RS1, p)

        @pl.when(i == 2)
        def _():
            reduce_near(pa, across_a, far_a, near_a, RS1, p, 3, False)

        @pl.when(i == 3)
        def _():
            reduce_near(pa, across_a, far_a, near_a, RS1, p, 1, False)
            reduce_near(pa, across_a, far_a, near_a, RS1, p, 3, True)
            reduce_near(pa, across_a, far_a, near_a, RS1, p, 1, True)
            if p == 1:
                resid_ready(0)
                gather_start(rg, AG2, 0)

        put(pa, across_a, RS1, dy, u, p, mixed[...], wo)
        if p == 0:
            @pl.when(i == 0)
            def _():
                reduce_far(pa, across_a, far_a, RS1, 0)

        return carry

    lax.fori_loop(0, NY, functools.partial(attention_step, 0), 0)
    lax.fori_loop(0, NY, functools.partial(attention_step, 1), 0)

    gather_forward(rg, AG2, 0)
    resid_ready(1)
    gather_start(rg, AG2, 1)
    for at in (2, 3, 4):
        weight_wait(at)

    owners = (owner(up_y), owner(down_y))

    def hand_over(p):
        for side in range(2):
            exchanged(across_b, RS2, p, 0, side)
        for cols in runs:
            total = rg[own + p, :, cols].astype(F32) + met(pb, across_b, p, 0, cols)
            share[p, :, cols] = total

        @pl.when(wrong == 1)
        def _():
            rounded[p] = share[p].astype(BF16)
            copy(rounded.at[p], handed.at[p], BACK + p, partner).start()

    def ffn_step(p, i, carry):
        dy = arrival(i)
        u = lax.rem(y + dy, NY)

        @pl.when(i == 1)
        def _():
            gather_near(rg, AG2, p)
            if p == 0:
                gather_forward(rg, AG2, 1)

        @pl.when(i == 3)
        def _():
            gather_far(rg, AG2, p)

        crossed(rg, AG2, dy, p)
        rows_in = jnp.concatenate([rg[4 * u + p], rg[4 * u + 2 + p]], axis=0)
        normed[:rows_now, :] = norm_rows(rows_in, fgain_ref[...])
        rows_in = normed[:rows_now, :]
        gate = jnp.dot(rows_in, wg[...], preferred_element_type=F32)
        lift = jnp.dot(rows_in, wu[...], preferred_element_type=F32)
        hidden = (gate / (1.0 + jnp.exp(-gate)) * lift).astype(BF16)
        put(pb, across_b, RS2, dy, u, p, hidden, wd)
        if p == 1:
            @pl.when(i == 0)
            def _():
                reduce_far(pb, across_b, far_b, RS2, 0)

        @pl.when(i == 2)
        def _():
            reduce_near(pb, across_b, far_b, near_b, RS2, p, 3, False, owners)
            hand_over(p)
            if p == 1:
                reduce_near(pb, across_b, far_b, near_b, RS2, 0, 3, True, owners)
                reduce_near(pb, across_b, far_b, near_b, RS2, 0, 1, True, owners)

        @pl.when(i == 3)
        def _():
            reduce_near(pb, across_b, far_b, near_b, RS2, p, 1, False, owners)

        return carry

    lax.fori_loop(0, NY, functools.partial(ffn_step, 0), 0)
    lax.fori_loop(0, NY, functools.partial(ffn_step, 1), 0)

    def finish(p):
        def result(cols, value):
            final[p, :, cols] = value

        @pl.when(wrong == 1)
        def _():
            arrived(handed.at[p], BACK + p)
            share[p] = handed[p].astype(F32)

        reduce_own(near_b, RS2, p, lambda cols: share[p, :, cols], result)

    reduce_far(pb, across_b, far_b, RS2, 1)
    finish(0)
    reduce_near(pb, across_b, far_b, near_b, RS2, 1, 3, True, owners)
    reduce_near(pb, across_b, far_b, near_b, RS2, 1, 1, True, owners)
    finish(1)

    for lo, size in tiles(width, 128):
        rows = jnp.concatenate([final[0, :, lo : lo + size], final[1, :, lo : lo + size]], axis=0)
        y_ref[lo : lo + size, :] = rows.T

    gather_sent(xg, AG1)
    gather_sent(rg, AG2)
    reduce_sent(pa, across_a, RS1)
    reduce_sent(pb, across_b, RS2)

    @pl.when(wrong == 0)
    def _():
        sent(segs, SEGS)
        weights_sent(True)

    @pl.when(wrong == 1)
    def _():
        weights_sent(False)
        for at, (src, dst) in enumerate(weights):
            for piece in range(PIECES[at][0]):
                sent(rows_of(dst, at, piece, parity), OVER_X + BEFORE[at] + piece)
        for p in range(2):
            for side in range(2):
                sent(run_of(xg, own + p, side), SWAP + 2 * p + side)
            sent(rounded.at[p], BACK + p)


def shards(
    activations, segment_ids, attn_gain, qkv_weight, out_weight, ffn_gain, gate_weight, up_weight, down_weight
):
    rows, width = activations.shape
    half, tokens = rows // 2, rows * 8
    chunk = 2 * rows
    vmem = pltpu.VMEM
    whole = pl.BlockSpec(memory_space=pltpu.VMEM)
    away = pl.BlockSpec(memory_space=pl.ANY)
    return pl.pallas_call(
        kernel,
        out_shape=pltpu.VMEM((width, rows), BF16),
        in_specs=[away, whole, whole, away, away, whole, away, away, away],
        out_specs=whole,
        scratch_shapes=[
            vmem((16, half, width), BF16),
            vmem((16, half, width), BF16),
            vmem((16, half, width), BF16),
            vmem((16, half, width), BF16),
            vmem((4, 2, half, width), BF16),
            vmem((4, 2, half, width), BF16),
            vmem((2, half, width), BF16),
            vmem((2, half, width), BF16),
            vmem((2, 2, half, width), BF16),
            vmem((2, 2, half, width), BF16),
            vmem(qkv_weight.shape, BF16),
            vmem(out_weight.shape[::-1], BF16),
            vmem(gate_weight.shape, BF16),
            vmem(up_weight.shape, BF16),
            vmem(down_weight.shape[::-1], BF16),
            vmem((2, NY, 2, half, Q_COLS), BF16),
            vmem((2, tokens, 128), BF16),
            vmem((2, tokens, 128), BF16),
            vmem((rows, Q_COLS), BF16),
            vmem((rows, tokens), F32),
            vmem((chunk, width), BF16),
            vmem((1, tokens), jnp.int32),
            vmem((2, half, width), BF16),
            vmem((2, half, width), F32),
            vmem((2, half, width), BF16),
            vmem((2, half, width), BF16),
            vmem((width, rows), BF16),
            vmem((2, half, width), BF16),
            pltpu.SemaphoreType.DMA((SLOTS,)),
            pltpu.SemaphoreType.DMA((SLOTS,)),
            pltpu.SemaphoreType.DMA((7,)),
        ],
        compiler_params=pltpu.CompilerParams(
            collective_id=0, has_side_effects=True, vmem_limit_bytes=64000000
        ),
    )(
        activations.T, segment_ids.reshape(1, tokens), attn_gain, qkv_weight, out_weight.T,
        ffn_gain, gate_weight, up_weight, down_weight.T,
    ).T


def solution(mesh):
    groups = mesh.shape["dp"] // 8
    torus = Mesh(mesh.devices.reshape(4, groups, 2, NY, 2), AXES)
    dp, tensor = ("x", "zh", "core"), ("y", "zl")
    in_specs = (
        P(dp + tensor, None), P(dp), P(), P(None, tensor), P(tensor, None), P(),
        P(None, tensor), P(None, tensor), P(tensor, None),
    )
    return jax.shard_map(
        shards, mesh=torus, in_specs=in_specs, out_specs=P(dp + tensor, None), check_vma=False
    )
```
